32 devices in a mesh: group: 2 (over y), expert: 16 (over z, x, core), token: 1.
Axes of the slice: x: 2, y: 2, z: 4, core: 2. Of those that a mesh axis runs over, the one named last changes fastest.
Arguments:
- tokens: bfloat16 [4096, 2048], P(('group', 'expert', 'token')), parts along dimension 0, may hold values from -6 to 6
- expert_ids: int32 [4096, 8], P(('group', 'expert', 'token')), parts along dimension 0, may hold values from 0 to 15, all different within a row; in each aligned block of 128 rows (0 to 127, 128 to 255, ...) at most 96 rows name the same one
- route_weights: float32 [4096, 8], P(('group', 'expert', 'token')), parts along dimension 0, may hold values from 0.05 to 1
- gate_up: bfloat16 [16, 2048, 768], P('expert', 'token'), may hold values from -0.125 to 0.125
- down_t: bfloat16 [16, 2048, 384], P('expert', 'token'), may hold values from -0.3125 to 0.3125
Outputs:
- moe_out: bfloat16 [4096, 2048], P(('group', 'expert', 'token')), parts along dimension 0
The draws below stay inside these ranges and needn't reach their ends.
There are 2 independent parts, one for each index of `group`. The reference program is written for one: setup_inputs(seed, part) draws one part's arguments, and reference() takes and returns one part's arrays. A program takes and returns all parts, laid end to end along the dimension named above; an argument that names none is the same for every part. Nothing has to cross between parts.
Inputs may be any that keep to these rules, and one draw needn't show every extreme that they name: `expert_ids`: each row names 8 different experts. Within the rows of one device (aligned blocks of 128 rows) no expert is named by more than 96 rows, a bound that some block reaches.
All inputs are finite; a program needn't handle non-finite values.
Results may differ from the reference program's by a relative error of at most 0.0058.
Values may be sent and summed in bfloat16 or wider, within the bound.
No kernel may reach another device: no remote copies, remote signals or barrier semaphores. Data moves between devices by JAX's collectives and lax.ppermute only.
A program may use at most 128 MiB of HBM per device.

```python
import math
import jax
import jax.numpy as jnp
import numpy as np
from jax import lax

D = 2048
FF = 384
TOPK = 8
TOK_DEV = 128
EXPERTS = 16
CAP = 96
TOKENS = 2048
N_EXPERT = 16
N_TOKEN = 1


def block_scale(own_key, extent, cuts, low, top_value):
    level, own = 1.0, jax.random.fold_in(own_key, 6)
    for dim, blocks in cuts:
        draws = jnp.exp(jax.random.uniform(jax.random.fold_in(own, dim), (blocks,), jnp.float32, low / len(cuts), top_value / len(cuts)))
        level = level * jnp.repeat(draws, extent[dim] // blocks).reshape([-1 if axis == dim else 1 for axis in range(len(extent))])
    return level


def shared_out(stream_key, own, number, rows, number_of, top, reach, slope):
    order = jax.random.permutation(stream_key, number_of)
    heavy_load, usual = load_shares(number_of, rows * top, reach, slope, True), load_shares(number_of, rows * top, reach, slope, False)
    places = jnp.arange(number_of)

    def named(lengths, rotation):
        used = int((lengths > 0).sum())
        fixed = max(1, used // 4)
        shifted = fixed + (places - fixed + rotation * (used - fixed)) % max(1, number_of - fixed)
        return jnp.zeros((number_of,), jnp.int32).at[order[jnp.where(places < fixed, places, shifted)]].set(jnp.asarray(lengths, jnp.int32))

    lengths = jnp.where(number % 4 == 0, named(heavy_load, number // 4), named(usual, number - number // 4 - 1))
    mixed = jax.random.permutation(jax.random.fold_in(own, 3), number_of)
    source_of, receiver = mixed[0:number_of // 2 * 2:2], mixed[1:number_of // 2 * 2:2]
    room = jnp.minimum(lengths[source_of] - 1, reach - lengths[receiver]) // 2
    room = jnp.where((source_of == order[0]) | (receiver == order[0]) | (lengths[receiver] == 0), 0, jnp.maximum(room, 0))
    shifted = jax.random.randint(jax.random.fold_in(own, 4), (number_of // 2,), 0, 1 << 20) % (room + 1)
    lengths = lengths.at[source_of].add(-shifted).at[receiver].add(shifted)
    labels = jnp.searchsorted(jnp.cumsum(lengths), jnp.arange(rows * top), side="right").astype(jnp.int32)
    listing = labels.reshape(top, rows).T
    listing = listing[jax.random.permutation(jax.random.fold_in(own, 1), rows)]
    rotation = jax.random.randint(jax.random.fold_in(own, 2), (rows, 1), 0, top)
    return jnp.take_along_axis(listing, (jnp.arange(top)[None, :] + rotation) % top, axis=1)


def load_shares(number_of, total, reach, lean, full):
    weights = [(1 << 20) // math.isqrt(grade ** lean) + 1 for grade in range(1, number_of + 1)]
    largest = reach if full else min(reach, max(-(-total // number_of), total * weights[0] // sum(weights)))
    least = 1 if total - largest >= number_of - 1 else 0
    given, spare = [largest] + [least] * (number_of - 1), total - largest - least * (number_of - 1)
    while spare > 0:
        movable = [i for i in range(1, number_of) if given[i] < largest] or [i for i in range(1, number_of) if given[i] < reach]
        mass, left = sum([weights[i] for i in movable]), spare
        for i in movable:
            extra = min(reach - given[i], max(1, left * weights[i] // mass), spare)
            given[i] = given[i] + extra
            spare = spare - extra
    return np.array(given)


def noise(own_key, dims, width, most, cuts=(), kind=jnp.bfloat16):
    loudness = block_scale(own_key, dims, cuts, -0.22, 0.18) if cuts else 1.0
    values = jax.random.normal(own_key, dims, jnp.float32) * width * loudness
    return jnp.minimum(jnp.maximum(values, -most), most).astype(kind)


def setup_inputs(seed: int = 0, part: int = 0) -> dict:
    seeds = jax.random.split(jax.random.key(seed), 6)
    own_keys = jax.random.split(jax.random.fold_in(seeds[5], part), 6)
    tokens = noise(own_keys[0], (TOKENS, D), 1.0, 6.0, ((0, 16),))
    expert_ids_keys = jax.random.split(jax.random.fold_in(own_keys[1], 1), TOKENS // TOK_DEV)
    expert_ids_turns = jax.random.permutation(jax.random.fold_in(own_keys[1], 3), TOKENS // TOK_DEV)
    expert_ids = jax.vmap(lambda own, number: shared_out(jax.random.fold_in(own_keys[1], 2), own, number, TOK_DEV, EXPERTS, TOPK, CAP, 2))(expert_ids_keys, expert_ids_turns).reshape((TOKENS, TOPK))
    route_weights = jnp.clip(0.05 + 0.95 * jax.random.uniform(own_keys[2], (TOKENS, TOPK), jnp.float32) ** block_scale(own_keys[2], (TOKENS, TOPK), ((0, 16),), -0.2, 0.2), 0.05, 1.0)
    gate_up = noise(seeds[3], (EXPERTS, D, 2 * FF), D ** -0.5, 0.125, ((0, 16),))
    down_t = noise(seeds[4], (EXPERTS, D, FF), FF ** -0.5, 0.3125, ((0, 16),))
    return dict(tokens=tokens, expert_ids=expert_ids, route_weights=route_weights, gate_up=gate_up, down_t=down_t)


def reference(tokens, expert_ids, route_weights, gate_up, down_t):
    flat_ids = expert_ids.reshape(-1).astype(jnp.int32)
    flat_weights = route_weights.reshape(-1)
    order = jnp.argsort(flat_ids, stable=True).astype(jnp.int32)
    max_rows = N_EXPERT * N_TOKEN * CAP
    padded = jnp.concatenate([order, jnp.zeros((max_rows,), jnp.int32)])
    counts = jnp.sum((flat_ids[None, :] == jnp.arange(EXPERTS, dtype=jnp.int32)[:, None]).astype(jnp.int32), axis=1).astype(jnp.int32)
    starts = (jnp.cumsum(counts) - counts).astype(jnp.int32)

    def step(total, expert):
        picks = lax.dynamic_slice_in_dim(padded, starts[expert], max_rows)
        live = jnp.arange(max_rows, dtype=jnp.int32) < counts[expert]
        owners = (picks // TOPK).astype(jnp.int32)
        rows = tokens[owners]
        pre = jnp.dot(rows, gate_up[expert], preferred_element_type=jnp.float32)
        hidden = (jax.nn.silu(pre[:, :FF]) * pre[:, FF:]).astype(jnp.bfloat16)
        outputs = lax.dot_general(hidden, down_t[expert], (((1,), (1,)), ((), ())), preferred_element_type=jnp.float32).astype(jnp.bfloat16)
        scale = jnp.where(live, flat_weights[picks], jnp.zeros((), flat_weights.dtype))
        total = total.at[owners].add(scale[:, None] * outputs.astype(total.dtype))
        return total, None

    total, _ = lax.scan(step, jnp.zeros((TOKENS, D), jnp.float32), jnp.arange(EXPERTS, dtype=jnp.int32))
    return total.astype(jnp.bfloat16)
```

```python
import functools

import jax
import jax.numpy as jnp
from jax import lax
from jax.experimental import pallas as pl
from jax.experimental.pallas import tpu as pltpu
from jax.sharding import PartitionSpec as P


def expert_apply(arrived, full_gate_up, full_down):
    shape = arrived.shape
    width = full_down.shape[2]
    rows = arrived.reshape(-1, shape[-1])
    pre = jnp.dot(rows, full_gate_up[0], preferred_element_type=jnp.float32)
    hidden = (jax.nn.silu(pre[:, :width]) * pre[:, width:]).astype(jnp.bfloat16)
    outputs = lax.dot_general(
        hidden, full_down[0], (((1,), (1,)), ((), ())), preferred_element_type=jnp.float32
    )
    return outputs.astype(jnp.bfloat16).reshape(shape)


def exchange_rows(tokens, expert_ids, route_weights, gate_up, down_t):
    tok_rows, choices_each = expert_ids.shape
    features = tokens.shape[1]
    num_experts = lax.axis_size("expert")
    slot_count = min(
        tok_rows, (3 * tok_rows * choices_each + 2 * num_experts - 1) // (2 * num_experts)
    )
    full_gate_up, full_down = (
        lax.all_gather(gate_up, "token", axis=1, tiled=True),
        lax.all_gather(down_t, "token", axis=1, tiled=True),
    )
    flat_ids = expert_ids.reshape(-1)
    onehot = (flat_ids[:, None] == jnp.arange(num_experts, dtype=jnp.int32)[None, :]).astype(
        jnp.int32
    )
    running = jnp.cumsum(onehot, axis=0)
    ranks = jnp.sum(running * onehot, axis=1) - 1
    slots = flat_ids * slot_count + ranks
    repeated = jnp.repeat(tokens, choices_each, axis=0)
    outgoing = jnp.zeros((num_experts * slot_count, features), jnp.bfloat16).at[slots].set(repeated)
    outgoing = outgoing.reshape(num_experts, slot_count, features)
    arrived = lax.all_to_all(outgoing, "expert", split_axis=0, concat_axis=0, tiled=True)
    served = expert_apply(arrived, full_gate_up, full_down)
    returned = lax.all_to_all(served, "expert", split_axis=0, concat_axis=0, tiled=True)
    picked = returned.reshape(num_experts * slot_count, features)[slots]
    picked = picked.reshape(tok_rows, choices_each, features)
    total = jnp.zeros((tok_rows, features), jnp.float32)
    for which in range(choices_each):
        total = total + route_weights[:, which : which + 1] * picked[:, which].astype(jnp.float32)
    return total.astype(jnp.bfloat16)


def chip_cycle(mesh):
    devices = mesh.devices[0, :, 0]
    chips = {}
    for index, device in enumerate(devices):
        chips.setdefault(tuple(getattr(device, "coords", (index // 2,))), []).append(index)
    coords = sorted(chips)
    wide = [d for d in range(len(coords[0])) if len({c[d] for c in coords}) > 1]
    if len(wide) == 2:
        wide.sort(key=lambda d: len({c[d] for c in coords}))
        short, long = wide
        turn = {v: i for i, v in enumerate(sorted({c[short] for c in coords}))}
        coords.sort(key=lambda c: (turn[c[short]], c[long] if turn[c[short]] % 2 == 0 else -c[long]))
    return [chips[c] for c in coords]


def two_experts(width, num_experts, own_ref, *refs):
    tokens, (gate_a, gate_b, down_a, down_b), outs = refs[:-6], refs[-6:-2], refs[-2:]
    features = down_a.shape[0]
    rows = jnp.concatenate([t[...] for t in tokens], axis=0)
    values, shares = rows[:, :features], rows[:, features:].astype(jnp.float32)
    lanes = lax.broadcasted_iota(jnp.int32, shares.shape, 1)
    total = None
    for which, (gate, down) in enumerate(((gate_a, down_a), (gate_b, down_b))):
        expert = own_ref[which]
        share = jnp.where((lanes == expert) | (lanes == expert + num_experts), shares, 0.0)
        share = jnp.sum(share, axis=1, keepdims=True)
        pre = jnp.dot(values, gate[...], preferred_element_type=jnp.float32)
        gated, up = pre[:, :width], pre[:, width:]
        hidden = (gated / (1.0 + jnp.exp(-gated)) * up * share).astype(jnp.bfloat16)
        part = lax.dot_general(
            hidden, down[...], (((1,), (1,)), ((), ())), preferred_element_type=jnp.float32
        )
        total = part if total is None else total + part
    half = outs[0].shape[0]
    outs[0][...] = total[:half]
    outs[1][...] = total[half:]


def ring(stops, tokens, expert_ids, route_weights, gate_up, down_t):
    tok_rows, features = tokens.shape
    num_experts, width = lax.axis_size("expert"), down_t.shape[2]
    count, half = len(stops), tok_rows // 2
    members = len(stops[0])
    me = lax.axis_index("expert")
    partner_of = [0] * num_experts
    for stop in stops:
        for place, member in enumerate(stop):
            partner_of[member] = stop[(place + 1) % members]
    forward = [
        (stops[s][m], stops[(s + 1) % count][m]) for s in range(count) for m in range(members)
    ]
    backward = [(b, a) for a, b in forward]
    swap = list(enumerate(partner_of))
    own = jnp.stack([me, jnp.asarray(partner_of, jnp.int32)[me]]).astype(jnp.int32)

    experts = jnp.arange(num_experts, dtype=jnp.int32)
    share = jnp.sum(
        jnp.where(expert_ids[:, :, None] == experts, route_weights[:, :, None], 0.0), axis=1
    )
    high = lax.reduce_precision(share, 8, 7)
    low = (share - high).astype(jnp.bfloat16)
    pad = -2 * num_experts % 128
    carried = jnp.concatenate(
        [tokens, high.astype(jnp.bfloat16), low, jnp.zeros((tok_rows, pad), jnp.bfloat16)], axis=1
    )
    gate_a, down_a = gate_up[0], down_t[0]
    gate_b, down_b = (lax.ppermute(w, "expert", swap) for w in (gate_a, down_a))
    kernel = pl.pallas_call(
        functools.partial(two_experts, width, num_experts),
        out_shape=[jax.ShapeDtypeStruct((half, features), jnp.float32)] * 2,
        in_specs=[pl.BlockSpec(memory_space=pltpu.SMEM)]
        + [pl.BlockSpec(memory_space=pltpu.VMEM)] * 6,
        out_specs=[pl.BlockSpec(memory_space=pltpu.VMEM)] * 2,
        compiler_params=pltpu.CompilerParams(vmem_limit_bytes=40 * 1024 * 1024),
        name="two_experts",
    )
    serve = lambda t, u: kernel(own, t, u, gate_a, gate_b, down_a, down_b)
    right, left = carried[:half], carried[half:]
    home_right, home_left = serve(right, left)
    sum_right = sum_left = None
    for step in range(1, count):
        right = lax.ppermute(right, "expert", forward)
        left = lax.ppermute(left, "expert", backward)
        more_right, more_left = serve(right, left)
        if sum_right is not None:
            more_right += sum_right.astype(jnp.float32)
            more_left += sum_left.astype(jnp.float32)
        sum_right = lax.ppermute(more_right.astype(jnp.bfloat16), "expert", forward)
        sum_left = lax.ppermute(more_left.astype(jnp.bfloat16), "expert", backward)
    home_right += sum_right.astype(jnp.float32)
    home_left += sum_left.astype(jnp.float32)
    return jnp.concatenate([home_right, home_left], axis=0).astype(jnp.bfloat16)


def solution(mesh):
    placed = (
        P(("group", "expert", "token"), None),
        P(("group", "expert", "token"), None),
        P(("group", "expert", "token"), None),
        P("expert", "token", None),
        P("expert", "token", None),
    )

    def per_device(tokens, expert_ids, route_weights, gate_up, down_t):
        stops = chip_cycle(mesh)
        fits = mesh.shape["token"] == 1 and {len(s) for s in stops} == {2} and len(stops) > 1
        fits = fits and mesh.shape["expert"] <= 4 * expert_ids.shape[1] and gate_up.shape[0] == 1
        fits = fits and tokens.shape[0] % 16 == 0 and tokens.shape[1] % 128 == 0
        if fits:
            return ring(stops, tokens, expert_ids, route_weights, gate_up, down_t)
        return exchange_rows(tokens, expert_ids, route_weights, gate_up, down_t)

    return jax.shard_map(
        per_device,
        mesh=mesh,
        in_specs=placed,
        out_specs=P(("group", "expert", "token"), None),
        check_vma=False,
    )
```

```python
import functools

import jax
import jax.numpy as jnp
from jax import lax
from jax.experimental import pallas as pl
from jax.experimental.pallas import tpu as pltpu
from jax.sharding import PartitionSpec as P


def expert_apply(arrived, full_gate_up, full_down):
    shape = arrived.shape
    width = full_down.shape[2]
    rows = arrived.reshape(-1, shape[-1])
    pre = jnp.dot(rows, full_gate_up[0], preferred_element_type=jnp.float32)
    hidden = (jax.nn.silu(pre[:, :width]) * pre[:, width:]).astype(jnp.bfloat16)
    outputs = lax.dot_general(
        hidden, full_down[0], (((1,), (1,)), ((), ())), preferred_element_type=jnp.float32
    )
    return outputs.astype(jnp.bfloat16).reshape(shape)


def exchange_rows(tokens, expert_ids, route_weights, gate_up, down_t):
    tok_rows, choices_each = expert_ids.shape
    features = tokens.shape[1]
    num_experts = lax.axis_size("expert")
    slot_count = min(
        tok_rows, (3 * tok_rows * choices_each + 2 * num_experts - 1) // (2 * num_experts)
    )
    full_gate_up, full_down = (
        lax.all_gather(gate_up, "token", axis=1, tiled=True),
        lax.all_gather(down_t, "token", axis=1, tiled=True),
    )
    flat_ids = expert_ids.reshape(-1)
    onehot = (flat_ids[:, None] == jnp.arange(num_experts, dtype=jnp.int32)[None, :]).astype(
        jnp.int32
    )
    running = jnp.cumsum(onehot, axis=0)
    ranks = jnp.sum(running * onehot, axis=1) - 1
    slots = flat_ids * slot_count + ranks
    repeated = jnp.repeat(tokens, choices_each, axis=0)
    outgoing = jnp.zeros((num_experts * slot_count, features), jnp.bfloat16).at[slots].set(repeated)
    outgoing = outgoing.reshape(num_experts, slot_count, features)
    arrived = lax.all_to_all(outgoing, "expert", split_axis=0, concat_axis=0, tiled=True)
    served = expert_apply(arrived, full_gate_up, full_down)
    returned = lax.all_to_all(served, "expert", split_axis=0, concat_axis=0, tiled=True)
    picked = returned.reshape(num_experts * slot_count, features)[slots]
    picked = picked.reshape(tok_rows, choices_each, features)
    total = jnp.zeros((tok_rows, features), jnp.float32)
    for which in range(choices_each):
        total = total + route_weights[:, which : which + 1] * picked[:, which].astype(jnp.float32)
    return total.astype(jnp.bfloat16)


def chip_cycle(mesh):
    devices = mesh.devices[0, :, 0]
    chips = {}
    for index, device in enumerate(devices):
        chips.setdefault(tuple(getattr(device, "coords", (index // 2,))), []).append(index)
    coords = sorted(chips)
    wide = [d for d in range(len(coords[0])) if len({c[d] for c in coords}) > 1]
    if len(wide) == 2:
        wide.sort(key=lambda d: len({c[d] for c in coords}))
        short, long = wide
        turn = {v: i for i, v in enumerate(sorted({c[short] for c in coords}))}
        coords.sort(key=lambda c: (turn[c[short]], c[long] if turn[c[short]] % 2 == 0 else -c[long]))
    return [chips[c] for c in coords]


def two_experts(width, num_experts, own_ref, *refs):
    tokens, (gate_a, gate_b, down_a, down_b), outs = refs[:-6], refs[-6:-2], refs[-2:]
    features = down_a.shape[0]
    rows = jnp.concatenate([t[...] for t in tokens], axis=0)
    values, shares = rows[:, :features], rows[:, features:].astype(jnp.float32)
    lanes = lax.broadcasted_iota(jnp.int32, shares.shape, 1)
    total = None
    for which, (gate, down) in enumerate(((gate_a, down_a), (gate_b, down_b))):
        expert = own_ref[which]
        share = jnp.where((lanes == expert) | (lanes == expert + num_experts), shares, 0.0)
        share = jnp.sum(share, axis=1, keepdims=True)
        pre = jnp.dot(values, gate[...], preferred_element_type=jnp.float32)
        gated, up = pre[:, :width], pre[:, width:]
        hidden = (gated / (1.0 + jnp.exp(-gated)) * up * share).astype(jnp.bfloat16)
        part = lax.dot_general(
            hidden, down[...], (((1,), (1,)), ((), ())), preferred_element_type=jnp.float32
        )
        total = part if total is None else total + part
    half = outs[0].shape[0]
    outs[0][...] = total[:half]
    outs[1][...] = total[half:]


def ring(stops, tokens, expert_ids, route_weights, gate_up, down_t):
    tok_rows, features = tokens.shape
    num_experts, width = lax.axis_size("expert"), down_t.shape[2]
    count, half = len(stops), tok_rows // 2
    members = len(stops[0])
    me = lax.axis_index("expert")
    partner_of = [0] * num_experts
    for stop in stops:
        for place, member in enumerate(stop):
            partner_of[member] = stop[(place + 1) % members]
    forward = [
        (stops[s][m], stops[(s + 1) % count][m]) for s in range(count) for m in range(members)
    ]
    backward = [(b, a) for a, b in forward]
    swap = list(enumerate(partner_of))
    own = jnp.stack([me, jnp.asarray(partner_of, jnp.int32)[me]]).astype(jnp.int32)

    experts = jnp.arange(num_experts, dtype=jnp.int32)
    share = jnp.sum(
        jnp.where(expert_ids[:, :, None] == experts, route_weights[:, :, None], 0.0), axis=1
    )
    high = lax.reduce_precision(share, 8, 7)
    low = (share - high).astype(jnp.bfloat16)
    pad = -2 * num_experts % 128
    carried = jnp.concatenate(
        [tokens, high.astype(jnp.bfloat16), low, jnp.zeros((tok_rows, pad), jnp.bfloat16)], axis=1
    )
    gate_a, down_a = gate_up[0], down_t[0]
    gate_b, down_b = (lax.ppermute(w, "expert", swap) for w in (gate_a, down_a))
    kernel = pl.pallas_call(
        functools.partial(two_experts, width, num_experts),
        out_shape=[jax.ShapeDtypeStruct((half, features), jnp.float32)] * 2,
        in_specs=[pl.BlockSpec(memory_space=pltpu.SMEM)]
        + [pl.BlockSpec(memory_space=pltpu.VMEM)] * 6,
        out_specs=[pl.BlockSpec(memory_space=pltpu.VMEM)] * 2,
        compiler_params=pltpu.CompilerParams(vmem_limit_bytes=40 * 1024 * 1024),
        name="two_experts",
    )
    serve = lambda t, u: kernel(own, t, u, gate_a, gate_b, down_a, down_b)
    right, left = carried[:half], carried[half:]
    home = (right, left)
    right = lax.ppermute(right, "expert", forward)
    left = lax.ppermute(left, "expert", backward)
    sum_right = sum_left = None
    for step in range(1, count):
        here_right, here_left = right, left
        if step < count - 1:
            right = lax.ppermute(right, "expert", forward)
            left = lax.ppermute(left, "expert", backward)
        more_right, more_left = serve(here_right, here_left)
        right, left, _, _ = lax.optimization_barrier((right, left, more_right, more_left))
        if sum_right is not None:
            more_right += sum_right.astype(jnp.float32)
            more_left += sum_left.astype(jnp.float32)
        sum_right = lax.ppermute(more_right.astype(jnp.bfloat16), "expert", forward)
        sum_left = lax.ppermute(more_left.astype(jnp.bfloat16), "expert", backward)
    home_right, home_left = serve(*home)
    home_right += sum_right.astype(jnp.float32)
    home_left += sum_left.astype(jnp.float32)
    return jnp.concatenate([home_right, home_left], axis=0).astype(jnp.bfloat16)


def solution(mesh):
    placed = (
        P(("group", "expert", "token"), None),
        P(("group", "expert", "token"), None),
        P(("group", "expert", "token"), None),
        P("expert", "token", None),
        P("expert", "token", None),
    )

    def per_device(tokens, expert_ids, route_weights, gate_up, down_t):
        stops = chip_cycle(mesh)
        fits = mesh.shape["token"] == 1 and {len(s) for s in stops} == {2} and len(stops) > 1
        fits = fits and mesh.shape["expert"] <= 4 * expert_ids.shape[1] and gate_up.shape[0] == 1
        fits = fits and tokens.shape[0] % 16 == 0 and tokens.shape[1] % 128 == 0
        if fits:
            return ring(stops, tokens, expert_ids, route_weights, gate_up, down_t)
        return exchange_rows(tokens, expert_ids, route_weights, gate_up, down_t)

    return jax.shard_map(
        per_device,
        mesh=mesh,
        in_specs=placed,
        out_specs=P(("group", "expert", "token"), None),
        check_vma=False,
    )
```

```python
import functools

import jax
import jax.numpy as jnp
from jax import lax
from jax.experimental import pallas as pl
from jax.experimental.pallas import tpu as pltpu
from jax.sharding import PartitionSpec as P


def expert_apply(arrived, full_gate_up, full_down):
    shape = arrived.shape
    width = full_down.shape[2]
    rows = arrived.reshape(-1, shape[-1])
    pre = jnp.dot(rows, full_gate_up[0], preferred_element_type=jnp.float32)
    hidden = (jax.nn.silu(pre[:, :width]) * pre[:, width:]).astype(jnp.bfloat16)
    outputs = lax.dot_general(
        hidden, full_down[0], (((1,), (1,)), ((), ())), preferred_element_type=jnp.float32
    )
    return outputs.astype(jnp.bfloat16).reshape(shape)


def exchange_rows(tokens, expert_ids, route_weights, gate_up, down_t):
    tok_rows, choices_each = expert_ids.shape
    features = tokens.shape[1]
    num_experts = lax.axis_size("expert")
    slot_count = min(
        tok_rows, (3 * tok_rows * choices_each + 2 * num_experts - 1) // (2 * num_experts)
    )
    full_gate_up, full_down = (
        lax.all_gather(gate_up, "token", axis=1, tiled=True),
        lax.all_gather(down_t, "token", axis=1, tiled=True),
    )
    flat_ids = expert_ids.reshape(-1)
    onehot = (flat_ids[:, None] == jnp.arange(num_experts, dtype=jnp.int32)[None, :]).astype(
        jnp.int32
    )
    running = jnp.cumsum(onehot, axis=0)
    ranks = jnp.sum(running * onehot, axis=1) - 1
    slots = flat_ids * slot_count + ranks
    repeated = jnp.repeat(tokens, choices_each, axis=0)
    outgoing = jnp.zeros((num_experts * slot_count, features), jnp.bfloat16).at[slots].set(repeated)
    outgoing = outgoing.reshape(num_experts, slot_count, features)
    arrived = lax.all_to_all(outgoing, "expert", split_axis=0, concat_axis=0, tiled=True)
    served = expert_apply(arrived, full_gate_up, full_down)
    returned = lax.all_to_all(served, "expert", split_axis=0, concat_axis=0, tiled=True)
    picked = returned.reshape(num_experts * slot_count, features)[slots]
    picked = picked.reshape(tok_rows, choices_each, features)
    total = jnp.zeros((tok_rows, features), jnp.float32)
    for which in range(choices_each):
        total = total + route_weights[:, which : which + 1] * picked[:, which].astype(jnp.float32)
    return total.astype(jnp.bfloat16)


def chip_cycle(mesh):
    devices = mesh.devices[0, :, 0]
    chips = {}
    for index, device in enumerate(devices):
        chips.setdefault(tuple(getattr(device, "coords", (index // 2,))), []).append(index)
    coords = sorted(chips)
    wide = [d for d in range(len(coords[0])) if len({c[d] for c in coords}) > 1]
    if len(wide) == 2:
        wide.sort(key=lambda d: len({c[d] for c in coords}))
        short, long = wide
        turn = {v: i for i, v in enumerate(sorted({c[short] for c in coords}))}
        coords.sort(key=lambda c: (turn[c[short]], c[long] if turn[c[short]] % 2 == 0 else -c[long]))
    return [chips[c] for c in coords]


def two_experts(width, step, from_ref, tokens, shares, gate_a, gate_b, down_a, down_b, out):
    rows = tokens[...]
    share = jnp.transpose(shares[from_ref[step]])
    total = None
    for which, (gate, down) in enumerate(((gate_a, down_a), (gate_b, down_b))):
        pre = jnp.dot(rows, gate[...], preferred_element_type=jnp.float32)
        gated, up = pre[:, :width], pre[:, width:]
        hidden = gated / (1.0 + jnp.exp(-gated)) * up * share[:, which : which + 1]
        part = lax.dot_general(
            hidden.astype(jnp.bfloat16),
            down[...],
            (((1,), (1,)), ((), ())),
            preferred_element_type=jnp.float32,
        )
        total = part if total is None else total + part
    out[...] = total


def ring(stops, tokens, expert_ids, route_weights, gate_up, down_t):
    tok_rows, features = tokens.shape
    num_experts, width = lax.axis_size("expert"), down_t.shape[2]
    count = len(stops)
    partner = [0] * num_experts
    onward = [0] * num_experts
    source = [[0] * count for _ in range(num_experts)]
    for s in range(count):
        for place, turn in ((0, 1), (1, -1)):
            member = stops[s][place]
            partner[member] = stops[s][1 - place]
            onward[member] = stops[(s + turn) % count][place]
            source[member] = [stops[(s - turn * k) % count][place] for k in range(count)]
    hop = functools.partial(lax.ppermute, axis_name="expert", perm=list(enumerate(onward)))
    swap = functools.partial(lax.ppermute, axis_name="expert", perm=list(enumerate(partner)))

    gate_a, down_a = gate_up[0], down_t[0]
    away = hop(tokens)
    gate_b, down_b = swap(gate_a), swap(down_a)
    experts = jnp.arange(num_experts, dtype=jnp.int32)[:, None]
    ids, weights = expert_ids.T, route_weights.T
    share = sum(
        jnp.where(ids[k] == experts, weights[k], 0.0) for k in range(expert_ids.shape[1])
    )
    share = jnp.stack([share, share[jnp.asarray(partner)]], axis=1)
    shares = lax.all_to_all(share, "expert", split_axis=0, concat_axis=0, tiled=True)
    sources = jnp.asarray(source, jnp.int32)[lax.axis_index("expert")]

    def serve(rows, step):
        return pl.pallas_call(
            functools.partial(two_experts, width, step),
            out_shape=jax.ShapeDtypeStruct((tok_rows, features), jnp.float32),
            in_specs=[pl.BlockSpec(memory_space=pltpu.SMEM)]
            + [pl.BlockSpec(memory_space=pltpu.VMEM)] * 6,
            out_specs=pl.BlockSpec(memory_space=pltpu.VMEM),
            compiler_params=pltpu.CompilerParams(vmem_limit_bytes=40 * 1024 * 1024),
            name="two_experts",
        )(sources, rows, shares, gate_a, gate_b, down_a, down_b)

    total = None
    for step in range(1, count):
        here = away
        if step < count - 1:
            away = hop(away)
        more = serve(here, step)
        away, _ = lax.optimization_barrier((away, more))
        if total is not None:
            more += total.astype(jnp.float32)
        total = hop(more.astype(jnp.bfloat16))
    return (serve(tokens, 0) + total.astype(jnp.float32)).astype(jnp.bfloat16)


def solution(mesh):
    placed = (
        P(("group", "expert", "token"), None),
        P(("group", "expert", "token"), None),
        P(("group", "expert", "token"), None),
        P("expert", "token", None),
        P("expert", "token", None),
    )

    def per_device(tokens, expert_ids, route_weights, gate_up, down_t):
        stops = chip_cycle(mesh)
        fits = mesh.shape["token"] == 1 and {len(s) for s in stops} == {2} and len(stops) > 1
        fits = fits and mesh.shape["expert"] <= 4 * expert_ids.shape[1] and gate_up.shape[0] == 1
        fits = fits and tokens.shape[0] % 128 == 0 and tokens.shape[1] % 128 == 0
        if fits:
            return ring(stops, tokens, expert_ids, route_weights, gate_up, down_t)
        return exchange_rows(tokens, expert_ids, route_weights, gate_up, down_t)

    return jax.shard_map(
        per_device,
        mesh=mesh,
        in_specs=placed,
        out_specs=P(("group", "expert", "token"), None),
        check_vma=False,
    )
```

```python
import functools

import jax
import jax.numpy as jnp
from jax import lax
from jax.experimental import pallas as pl
from jax.experimental.pallas import tpu as pltpu
from jax.sharding import PartitionSpec as P


def expert_apply(arrived, full_gate_up, full_down):
    shape = arrived.shape
    width = full_down.shape[2]
    rows = arrived.reshape(-1, shape[-1])
    pre = jnp.dot(rows, full_gate_up[0], preferred_element_type=jnp.float32)
    hidden = (jax.nn.silu(pre[:, :width]) * pre[:, width:]).astype(jnp.bfloat16)
    outputs = lax.dot_general(
        hidden, full_down[0], (((1,), (1,)), ((), ())), preferred_element_type=jnp.float32
    )
    return outputs.astype(jnp.bfloat16).reshape(shape)


def exchange_rows(tokens, expert_ids, route_weights, gate_up, down_t):
    tok_rows, choices_each = expert_ids.shape
    features = tokens.shape[1]
    num_experts = lax.axis_size("expert")
    slot_count = min(
        tok_rows, (3 * tok_rows * choices_each + 2 * num_experts - 1) // (2 * num_experts)
    )
    full_gate_up, full_down = (
        lax.all_gather(gate_up, "token", axis=1, tiled=True),
        lax.all_gather(down_t, "token", axis=1, tiled=True),
    )
    flat_ids = expert_ids.reshape(-1)
    onehot = (flat_ids[:, None] == jnp.arange(num_experts, dtype=jnp.int32)[None, :]).astype(
        jnp.int32
    )
    running = jnp.cumsum(onehot, axis=0)
    ranks = jnp.sum(running * onehot, axis=1) - 1
    slots = flat_ids * slot_count + ranks
    repeated = jnp.repeat(tokens, choices_each, axis=0)
    outgoing = jnp.zeros((num_experts * slot_count, features), jnp.bfloat16).at[slots].set(repeated)
    outgoing = outgoing.reshape(num_experts, slot_count, features)
    arrived = lax.all_to_all(outgoing, "expert", split_axis=0, concat_axis=0, tiled=True)
    served = expert_apply(arrived, full_gate_up, full_down)
    returned = lax.all_to_all(served, "expert", split_axis=0, concat_axis=0, tiled=True)
    picked = returned.reshape(num_experts * slot_count, features)[slots]
    picked = picked.reshape(tok_rows, choices_each, features)
    total = jnp.zeros((tok_rows, features), jnp.float32)
    for which in range(choices_each):
        total = total + route_weights[:, which : which + 1] * picked[:, which].astype(jnp.float32)
    return total.astype(jnp.bfloat16)


def chip_cycle(mesh):
    devices = mesh.devices[0, :, 0]
    chips = {}
    for index, device in enumerate(devices):
        chips.setdefault(tuple(getattr(device, "coords", (index // 2,))), []).append(index)
    coords = sorted(chips)
    wide = [d for d in range(len(coords[0])) if len({c[d] for c in coords}) > 1]
    if len(wide) == 2:
        wide.sort(key=lambda d: len({c[d] for c in coords}))
        short, long = wide
        turn = {v: i for i, v in enumerate(sorted({c[short] for c in coords}))}
        coords.sort(key=lambda c: (turn[c[short]], c[long] if turn[c[short]] % 2 == 0 else -c[long]))
    return [chips[c] for c in coords]


def serve_rows(width, step, picks, from_ref, *refs):
    outs = refs[-2:]
    rows = jnp.concatenate([refs[0][...], refs[1][...]], axis=0)
    share = jnp.transpose(refs[2][from_ref[step]])
    total = None
    for place, which in enumerate(picks):
        gate, down = refs[3 + 2 * place], refs[4 + 2 * place]
        pre = jnp.dot(rows, gate[...], preferred_element_type=jnp.float32)
        gated, up = pre[:, :width], pre[:, width:]
        hidden = gated / (1.0 + jnp.exp(-gated)) * up * share[:, which : which + 1]
        part = lax.dot_general(
            hidden.astype(jnp.bfloat16),
            down[...],
            (((1,), (1,)), ((), ())),
            preferred_element_type=jnp.float32,
        )
        total = part if total is None else total + part
    half = outs[0].shape[0]
    outs[0][...] = total[:half]
    outs[1][...] = total[half:]


def ring(stops, tokens, expert_ids, route_weights, gate_up, down_t):
    tok_rows, features = tokens.shape
    num_experts, width = lax.axis_size("expert"), down_t.shape[2]
    count, half = len(stops), tok_rows // 2
    lead = 3
    partner = [0] * num_experts
    onward = [0] * num_experts
    source = [[0] * count for _ in range(num_experts)]
    for s in range(count):
        for place, turn in ((0, 1), (1, -1)):
            member = stops[s][place]
            partner[member] = stops[s][1 - place]
            onward[member] = stops[(s + turn) % count][place]
            source[member] = [stops[(s - turn * k) % count][place] for k in range(count)]
    swap = functools.partial(lax.ppermute, axis_name="expert", perm=list(enumerate(partner)))

    def hop(pair):
        return tuple(lax.ppermute(x, "expert", list(enumerate(onward))) for x in pair)

    def after(arrays, *others):
        return tuple(lax.optimization_barrier((x, others))[0] for x in arrays)

    own = (tokens[:half], tokens[half:])
    arrived = [own, hop(own)]
    weights = [(gate_up[0], down_t[0])]
    weights.append(tuple(swap(w) for w in weights[0]))
    experts = jnp.asarray([[e, partner[e]] for e in range(num_experts)], jnp.int32)
    share = jnp.sum(
        jnp.where(expert_ids.T == experts[:, :, None, None], route_weights.T, 0.0), axis=2
    )
    shares = lax.all_to_all(
        *after((share,), *arrived[1]), "expert", split_axis=0, concat_axis=0, tiled=True
    )
    sources = jnp.asarray(source, jnp.int32)[lax.axis_index("expert")]

    def serve(pair, step, table, picks):
        return pl.pallas_call(
            functools.partial(serve_rows, width, step, picks),
            out_shape=[jax.ShapeDtypeStruct((half, features), jnp.float32)] * 2,
            in_specs=[pl.BlockSpec(memory_space=pltpu.SMEM)]
            + [pl.BlockSpec(memory_space=pltpu.VMEM)] * (3 + 2 * len(picks)),
            out_specs=[pl.BlockSpec(memory_space=pltpu.VMEM)] * 2,
            compiler_params=pltpu.CompilerParams(vmem_limit_bytes=16 * 1024 * 1024),
            name="serve_rows",
        )(sources, *pair, table, *(w for which in picks for w in weights[which]))

    def plus(pair, more):
        return tuple(x + y.astype(jnp.float32) for x, y in zip(pair, more))

    def rounded(pair):
        return tuple(x.astype(jnp.bfloat16) for x in pair)

    home = serve(own, 0, share, (0,))
    for step in range(2, min(lead, count - 1) + 1):
        arrived.append(hop(arrived[-1] if step == 2 else after(arrived[-1], *home)))
    total = None
    for step in range(1, count):
        more = serve(arrived[step], step, shares, (0, 1))
        if step + lead < count:
            arrived.append(hop(after(arrived[-1], *more)))
        total = hop(rounded(more if total is None else plus(more, total)))
    home = plus(home, serve(own, 0, share, (1,)))
    return jnp.concatenate(rounded(plus(home, total)), axis=0)


def solution(mesh):
    placed = (
        P(("group", "expert", "token"), None),
        P(("group", "expert", "token"), None),
        P(("group", "expert", "token"), None),
        P("expert", "token", None),
        P("expert", "token", None),
    )

    def per_device(tokens, expert_ids, route_weights, gate_up, down_t):
        stops = chip_cycle(mesh)
        fits = mesh.shape["token"] == 1 and {len(s) for s in stops} == {2} and len(stops) > 1
        fits = fits and mesh.shape["expert"] <= 4 * expert_ids.shape[1] and gate_up.shape[0] == 1
        fits = fits and tokens.shape[0] % 128 == 0 and tokens.shape[1] % 128 == 0
        if fits:
            return ring(stops, tokens, expert_ids, route_weights, gate_up, down_t)
        return exchange_rows(tokens, expert_ids, route_weights, gate_up, down_t)

    return jax.shard_map(
        per_device,
        mesh=mesh,
        in_specs=placed,
        out_specs=P(("group", "expert", "token"), None),
        check_vma=False,
    )
```

```python
import functools

import jax
import jax.numpy as jnp
from jax import lax
from jax.experimental import pallas as pl
from jax.experimental.pallas import tpu as pltpu
from jax.sharding import PartitionSpec as P


def expert_apply(arrived, full_gate_up, full_down):
    shape = arrived.shape
    width = full_down.shape[2]
    rows = arrived.reshape(-1, shape[-1])
    pre = jnp.dot(rows, full_gate_up[0], preferred_element_type=jnp.float32)
    hidden = (jax.nn.silu(pre[:, :width]) * pre[:, width:]).astype(jnp.bfloat16)
    outputs = lax.dot_general(
        hidden, full_down[0], (((1,), (1,)), ((), ())), preferred_element_type=jnp.float32
    )
    return outputs.astype(jnp.bfloat16).reshape(shape)


def exchange_rows(tokens, expert_ids, route_weights, gate_up, down_t):
    tok_rows, choices_each = expert_ids.shape
    features = tokens.shape[1]
    num_experts = lax.axis_size("expert")
    slot_count = min(
        tok_rows, (3 * tok_rows * choices_each + 2 * num_experts - 1) // (2 * num_experts)
    )
    full_gate_up, full_down = (
        lax.all_gather(gate_up, "token", axis=1, tiled=True),
        lax.all_gather(down_t, "token", axis=1, tiled=True),
    )
    flat_ids = expert_ids.reshape(-1)
    onehot = (flat_ids[:, None] == jnp.arange(num_experts, dtype=jnp.int32)[None, :]).astype(
        jnp.int32
    )
    running = jnp.cumsum(onehot, axis=0)
    ranks = jnp.sum(running * onehot, axis=1) - 1
    slots = flat_ids * slot_count + ranks
    repeated = jnp.repeat(tokens, choices_each, axis=0)
    outgoing = jnp.zeros((num_experts * slot_count, features), jnp.bfloat16).at[slots].set(repeated)
    outgoing = outgoing.reshape(num_experts, slot_count, features)
    arrived = lax.all_to_all(outgoing, "expert", split_axis=0, concat_axis=0, tiled=True)
    served = expert_apply(arrived, full_gate_up, full_down)
    returned = lax.all_to_all(served, "expert", split_axis=0, concat_axis=0, tiled=True)
    picked = returned.reshape(num_experts * slot_count, features)[slots]
    picked = picked.reshape(tok_rows, choices_each, features)
    total = jnp.zeros((tok_rows, features), jnp.float32)
    for which in range(choices_each):
        total = total + route_weights[:, which : which + 1] * picked[:, which].astype(jnp.float32)
    return total.astype(jnp.bfloat16)


def chip_cycle(mesh):
    devices = mesh.devices[0, :, 0]
    chips = {}
    for index, device in enumerate(devices):
        chips.setdefault(tuple(getattr(device, "coords", (index // 2,))), []).append(index)
    coords = sorted(chips)
    wide = [d for d in range(len(coords[0])) if len({c[d] for c in coords}) > 1]
    if len(wide) == 2:
        wide.sort(key=lambda d: len({c[d] for c in coords}))
        short, long = wide
        turn = {v: i for i, v in enumerate(sorted({c[short] for c in coords}))}
        coords.sort(key=lambda c: (turn[c[short]], c[long] if turn[c[short]] % 2 == 0 else -c[long]))
    return [chips[c] for c in coords]


def pack_rows(tokens, ids, weights, out):
    tok_rows = tokens.shape[0]
    out[:tok_rows] = tokens[...]
    spare = out.shape[0] - tok_rows
    place = lax.broadcasted_iota(jnp.int32, (spare, tok_rows), 0)
    for expert in range(out.shape[1] // tok_rows):
        share = jnp.sum(jnp.where(ids[...] == expert, weights[...], 0.0), axis=0, keepdims=True)
        high = share.astype(jnp.bfloat16).astype(jnp.float32)
        both = jnp.where(place == 0, high, jnp.where(place == 1, share - high, 0.0))
        out[tok_rows:, expert * tok_rows : (expert + 1) * tok_rows] = both.astype(jnp.bfloat16)


def serve_rows(width, picks, experts_ref, packed, *refs):
    out = refs[-1]
    tok_rows = out.shape[0]
    rows = packed[:tok_rows]
    total = None
    for place, which in enumerate(picks):
        gate, down = refs[2 * place], refs[2 * place + 1]
        lane = pl.multiple_of(experts_ref[which] * tok_rows, tok_rows)
        share = packed[tok_rows:, pl.ds(lane, tok_rows)].astype(jnp.float32)
        share = jnp.sum(jnp.transpose(share), axis=1, keepdims=True)
        pre = jnp.dot(rows, gate[...], preferred_element_type=jnp.float32)
        gated, up = pre[:, :width], pre[:, width:]
        hidden = gated / (1.0 + jnp.exp(-gated)) * up * share
        part = lax.dot_general(
            hidden.astype(jnp.bfloat16),
            down[...],
            (((1,), (1,)), ((), ())),
            preferred_element_type=jnp.float32,
        )
        total = part if total is None else total + part
    out[...] = total


def ring(stops, tokens, expert_ids, route_weights, gate_up, down_t):
    tok_rows, features = tokens.shape
    num_experts, width = lax.axis_size("expert"), down_t.shape[2]
    count = len(stops)
    partner = [0] * num_experts
    onward = [0] * num_experts
    for s in range(count):
        for place, turn in ((0, 1), (1, -1)):
            partner[stops[s][place]] = stops[s][1 - place]
            onward[stops[s][place]] = stops[(s + turn) % count][place]
    hop = functools.partial(lax.ppermute, axis_name="expert", perm=list(enumerate(onward)))
    swap = functools.partial(lax.ppermute, axis_name="expert", perm=list(enumerate(partner)))
    whole = pl.BlockSpec(memory_space=pltpu.VMEM)

    packed = pl.pallas_call(
        pack_rows,
        out_shape=jax.ShapeDtypeStruct((tok_rows + 8, features), jnp.bfloat16),
        in_specs=[whole] * 3,
        out_specs=whole,
        name="pack_rows",
    )(tokens, expert_ids.T, route_weights.T)
    away = hop(packed)
    weights = [(gate_up[0], down_t[0])]
    weights.append(tuple(swap(w) for w in weights[0]))
    both = [[e, partner[e]] for e in range(num_experts)]
    both = jnp.asarray(both, jnp.int32)[lax.axis_index("expert")]

    def serve(rows, picks):
        return pl.pallas_call(
            functools.partial(serve_rows, width, picks),
            out_shape=jax.ShapeDtypeStruct((tok_rows, features), jnp.float32),
            in_specs=[pl.BlockSpec(memory_space=pltpu.SMEM)] + [whole] * (1 + 2 * len(picks)),
            out_specs=whole,
            compiler_params=pltpu.CompilerParams(vmem_limit_bytes=40 * 1024 * 1024),
            name="serve_rows",
        )(both, rows, *(w for which in picks for w in weights[which]))

    home = serve(packed, (0,))
    away, _ = lax.optimization_barrier((away, home))
    total = None
    for step in range(1, count):
        here = away
        if step < count - 1:
            away = hop(away)
        more = serve(here, (0, 1))
        away, _ = lax.optimization_barrier((away, more))
        if total is not None:
            more += total.astype(jnp.float32)
        total = hop(more.astype(jnp.bfloat16))
    home += serve(packed, (1,))
    return (home + total.astype(jnp.float32)).astype(jnp.bfloat16)


def solution(mesh):
    placed = (
        P(("group", "expert", "token"), None),
        P(("group", "expert", "token"), None),
        P(("group", "expert", "token"), None),
        P("expert", "token", None),
        P("expert", "token", None),
    )

    def per_device(tokens, expert_ids, route_weights, gate_up, down_t):
        stops = chip_cycle(mesh)
        fits = mesh.shape["token"] == 1 and {len(s) for s in stops} == {2} and len(stops) > 1
        fits = fits and mesh.shape["expert"] <= 4 * expert_ids.shape[1] and gate_up.shape[0] == 1
        fits = fits and tokens.shape[0] % 128 == 0
        fits = fits and tokens.shape[0] * mesh.shape["expert"] == tokens.shape[1]
        if fits:
            return ring(stops, tokens, expert_ids, route_weights, gate_up, down_t)
        return exchange_rows(tokens, expert_ids, route_weights, gate_up, down_t)

    return jax.shard_map(
        per_device,
        mesh=mesh,
        in_specs=placed,
        out_specs=P(("group", "expert", "token"), None),
        check_vma=False,
    )
```

```python
import functools

import jax
import jax.numpy as jnp
from jax import lax
from jax.experimental import pallas as pl
from jax.experimental.pallas import tpu as pltpu
from jax.sharding import PartitionSpec as P


def expert_apply(arrived, full_gate_up, full_down):
    shape = arrived.shape
    width = full_down.shape[2]
    rows = arrived.reshape(-1, shape[-1])
    pre = jnp.dot(rows, full_gate_up[0], preferred_element_type=jnp.float32)
    hidden = (jax.nn.silu(pre[:, :width]) * pre[:, width:]).astype(jnp.bfloat16)
    outputs = lax.dot_general(
        hidden, full_down[0], (((1,), (1,)), ((), ())), preferred_element_type=jnp.float32
    )
    return outputs.astype(jnp.bfloat16).reshape(shape)


def exchange_rows(tokens, expert_ids, route_weights, gate_up, down_t):
    tok_rows, choices_each = expert_ids.shape
    features = tokens.shape[1]
    num_experts = lax.axis_size("expert")
    slot_count = min(
        tok_rows, (3 * tok_rows * choices_each + 2 * num_experts - 1) // (2 * num_experts)
    )
    full_gate_up, full_down = (
        lax.all_gather(gate_up, "token", axis=1, tiled=True),
        lax.all_gather(down_t, "token", axis=1, tiled=True),
    )
    flat_ids = expert_ids.reshape(-1)
    onehot = (flat_ids[:, None] == jnp.arange(num_experts, dtype=jnp.int32)[None, :]).astype(
        jnp.int32
    )
    running = jnp.cumsum(onehot, axis=0)
    ranks = jnp.sum(running * onehot, axis=1) - 1
    slots = flat_ids * slot_count + ranks
    repeated = jnp.repeat(tokens, choices_each, axis=0)
    outgoing = jnp.zeros((num_experts * slot_count, features), jnp.bfloat16).at[slots].set(repeated)
    outgoing = outgoing.reshape(num_experts, slot_count, features)
    arrived = lax.all_to_all(outgoing, "expert", split_axis=0, concat_axis=0, tiled=True)
    served = expert_apply(arrived, full_gate_up, full_down)
    returned = lax.all_to_all(served, "expert", split_axis=0, concat_axis=0, tiled=True)
    picked = returned.reshape(num_experts * slot_count, features)[slots]
    picked = picked.reshape(tok_rows, choices_each, features)
    total = jnp.zeros((tok_rows, features), jnp.float32)
    for which in range(choices_each):
        total = total + route_weights[:, which : which + 1] * picked[:, which].astype(jnp.float32)
    return total.astype(jnp.bfloat16)


def chip_cycle(mesh):
    devices = mesh.devices[0, :, 0]
    chips = {}
    for index, device in enumerate(devices):
        chips.setdefault(tuple(getattr(device, "coords", (index // 2,))), []).append(index)
    coords = sorted(chips)
    wide = [d for d in range(len(coords[0])) if len({c[d] for c in coords}) > 1]
    if len(wide) == 2:
        wide.sort(key=lambda d: len({c[d] for c in coords}))
        short, long = wide
        turn = {v: i for i, v in enumerate(sorted({c[short] for c in coords}))}
        coords.sort(key=lambda c: (turn[c[short]], c[long] if turn[c[short]] % 2 == 0 else -c[long]))
    return [chips[c] for c in coords]


LANES = 128


def pack_rows(num_experts, *refs):
    far, out, near, done = refs[:3], refs[3], refs[4:7], refs[7]
    copies = [pltpu.make_async_copy(a, b, done.at[i]) for i, (a, b) in enumerate(zip(far, near))]
    for copy in copies:
        copy.start()
    for copy in copies:
        copy.wait()
    tokens, ids, weights = near
    tok_rows, features = tokens.shape
    for start in range(0, features, LANES):
        at = start // LANES * tok_rows
        out[at : at + tok_rows] = tokens[:, start : start + LANES]
    place = lax.broadcasted_iota(jnp.int32, (num_experts, tok_rows), 0)
    share = jnp.zeros(place.shape, jnp.float32)
    for choice in range(ids.shape[0]):
        named = ids[choice : choice + 1] == place
        share += jnp.where(named, weights[choice : choice + 1], 0.0)
    high = share.astype(jnp.bfloat16).astype(jnp.float32)
    both = jnp.concatenate([high, share - high], axis=0)
    out[features // LANES * tok_rows :] = both.astype(jnp.bfloat16)


def serve_rows(width, picks, partner, packed, *refs):
    out = refs[-1]
    tok_rows, features = out.shape
    blocks, num_experts = features // LANES, len(partner)
    rows = [packed[at * tok_rows : (at + 1) * tok_rows] for at in range(blocks)]
    rows = jnp.concatenate(rows, axis=1)
    shares = jnp.transpose(packed[blocks * tok_rows :].astype(jnp.float32))
    lanes = lax.broadcasted_iota(jnp.int32, shares.shape, 1)
    me = lax.axis_index("expert")
    other = sum(jnp.where(me == e, partner[e], 0) for e in range(num_experts))
    total = None
    for place, which in enumerate(picks):
        gate, down = refs[2 * place], refs[2 * place + 1]
        expert = (me, other)[which]
        share = jnp.where((lanes == expert) | (lanes == expert + num_experts), shares, 0.0)
        share = jnp.sum(share, axis=1, keepdims=True)
        pre = jnp.dot(rows, gate[...], preferred_element_type=jnp.float32)
        gated, up = pre[:, :width], pre[:, width:]
        hidden = gated / (1.0 + jnp.exp(-gated)) * up * share
        part = lax.dot_general(
            hidden.astype(jnp.bfloat16),
            down[...],
            (((1,), (1,)), ((), ())),
            preferred_element_type=jnp.float32,
        )
        total = part if total is None else total + part
    out[...] = total


def ring(stops, tokens, expert_ids, route_weights, gate_up, down_t):
    tok_rows, features = tokens.shape
    num_experts, width = lax.axis_size("expert"), down_t.shape[2]
    count = len(stops)
    partner = [0] * num_experts
    onward = [0] * num_experts
    for s in range(count):
        for place, turn in ((0, 1), (1, -1)):
            partner[stops[s][place]] = stops[s][1 - place]
            onward[stops[s][place]] = stops[(s + turn) % count][place]
    hop = functools.partial(lax.ppermute, axis_name="expert", perm=list(enumerate(onward)))
    swap = functools.partial(lax.ppermute, axis_name="expert", perm=list(enumerate(partner)))
    whole = pl.BlockSpec(memory_space=pltpu.VMEM)

    given = (tokens, expert_ids.T, route_weights.T)
    packed = pl.pallas_call(
        functools.partial(pack_rows, num_experts),
        out_shape=jax.ShapeDtypeStruct(
            (features // LANES * tok_rows + 2 * num_experts, LANES), jnp.bfloat16
        ),
        in_specs=[pl.BlockSpec(memory_space=pl.ANY)] * 3,
        out_specs=whole,
        scratch_shapes=[pltpu.VMEM(x.shape, x.dtype) for x in given]
        + [pltpu.SemaphoreType.DMA((3,))],
        compiler_params=pltpu.CompilerParams(vmem_limit_bytes=8 * 1024 * 1024),
        name="pack_rows",
    )(*given)
    away = hop(packed)
    weights = [(gate_up[0], down_t[0])]
    weights.append(tuple(swap(w) for w in weights[0]))

    def serve(rows, picks):
        return pl.pallas_call(
            functools.partial(serve_rows, width, picks, partner),
            out_shape=jax.ShapeDtypeStruct((tok_rows, features), jnp.float32),
            in_specs=[whole] * (1 + 2 * len(picks)),
            out_specs=whole,
            compiler_params=pltpu.CompilerParams(vmem_limit_bytes=8 * 1024 * 1024),
            name="serve_rows",
        )(rows, *(w for which in picks for w in weights[which]))

    home = serve(packed, (0,))
    away, _ = lax.optimization_barrier((away, home))
    total = None
    for step in range(1, count):
        here = away
        if step < count - 1:
            away = hop(away)
        more = serve(here, (0, 1))
        away, _ = lax.optimization_barrier((away, more))
        if total is not None:
            more += total.astype(jnp.float32)
        total = hop(more.astype(jnp.bfloat16))
    home += serve(packed, (1,))
    return (home + total.astype(jnp.float32)).astype(jnp.bfloat16)


def solution(mesh):
    placed = (
        P(("group", "expert", "token"), None),
        P(("group", "expert", "token"), None),
        P(("group", "expert", "token"), None),
        P("expert", "token", None),
        P("expert", "token", None),
    )

    def per_device(tokens, expert_ids, route_weights, gate_up, down_t):
        stops = chip_cycle(mesh)
        fits = mesh.shape["token"] == 1 and {len(s) for s in stops} == {2} and len(stops) > 1
        fits = fits and mesh.shape["expert"] <= 4 * expert_ids.shape[1] and gate_up.shape[0] == 1
        fits = fits and tokens.shape[0] == LANES and tokens.shape[1] % LANES == 0
        if fits:
            return ring(stops, tokens, expert_ids, route_weights, gate_up, down_t)
        return exchange_rows(tokens, expert_ids, route_weights, gate_up, down_t)

    return jax.shard_map(
        per_device,
        mesh=mesh,
        in_specs=placed,
        out_specs=P(("group", "expert", "token"), None),
        check_vma=False,
    )
```

```python
import functools

import jax
import jax.numpy as jnp
from jax import lax
from jax.experimental import pallas as pl
from jax.experimental.pallas import tpu as pltpu
from jax.sharding import PartitionSpec as P


def expert_apply(arrived, full_gate_up, full_down):
    shape = arrived.shape
    width = full_down.shape[2]
    rows = arrived.reshape(-1, shape[-1])
    pre = jnp.dot(rows, full_gate_up[0], preferred_element_type=jnp.float32)
    hidden = (jax.nn.silu(pre[:, :width]) * pre[:, width:]).astype(jnp.bfloat16)
    outputs = lax.dot_general(
        hidden, full_down[0], (((1,), (1,)), ((), ())), preferred_element_type=jnp.float32
    )
    return outputs.astype(jnp.bfloat16).reshape(shape)


def exchange_rows(tokens, expert_ids, route_weights, gate_up, down_t):
    tok_rows, choices_each = expert_ids.shape
    features = tokens.shape[1]
    num_experts = lax.axis_size("expert")
    slot_count = min(
        tok_rows, (3 * tok_rows * choices_each + 2 * num_experts - 1) // (2 * num_experts)
    )
    full_gate_up, full_down = (
        lax.all_gather(gate_up, "token", axis=1, tiled=True),
        lax.all_gather(down_t, "token", axis=1, tiled=True),
    )
    flat_ids = expert_ids.reshape(-1)
    onehot = (flat_ids[:, None] == jnp.arange(num_experts, dtype=jnp.int32)[None, :]).astype(
        jnp.int32
    )
    running = jnp.cumsum(onehot, axis=0)
    ranks = jnp.sum(running * onehot, axis=1) - 1
    slots = flat_ids * slot_count + ranks
    repeated = jnp.repeat(tokens, choices_each, axis=0)
    outgoing = jnp.zeros((num_experts * slot_count, features), jnp.bfloat16).at[slots].set(repeated)
    outgoing = outgoing.reshape(num_experts, slot_count, features)
    arrived = lax.all_to_all(outgoing, "expert", split_axis=0, concat_axis=0, tiled=True)
    served = expert_apply(arrived, full_gate_up, full_down)
    returned = lax.all_to_all(served, "expert", split_axis=0, concat_axis=0, tiled=True)
    picked = returned.reshape(num_experts * slot_count, features)[slots]
    picked = picked.reshape(tok_rows, choices_each, features)
    total = jnp.zeros((tok_rows, features), jnp.float32)
    for which in range(choices_each):
        total = total + route_weights[:, which : which + 1] * picked[:, which].astype(jnp.float32)
    return total.astype(jnp.bfloat16)


def chip_cycle(mesh):
    devices = mesh.devices[0, :, 0]
    chips = {}
    for index, device in enumerate(devices):
        chips.setdefault(tuple(getattr(device, "coords", (index // 2,))), []).append(index)
    coords = sorted(chips)
    wide = [d for d in range(len(coords[0])) if len({c[d] for c in coords}) > 1]
    if len(wide) == 2:
        wide.sort(key=lambda d: len({c[d] for c in coords}))
        short, long = wide
        turn = {v: i for i, v in enumerate(sorted({c[short] for c in coords}))}
        coords.sort(key=lambda c: (turn[c[short]], c[long] if turn[c[short]] % 2 == 0 else -c[long]))
    return [chips[c] for c in coords]


LANES = 128


def pack_rows(num_experts, *refs):
    far, outs, near, done = refs[:3], refs[3:5], refs[5:8], refs[8]
    copies = [pltpu.make_async_copy(a, b, done.at[i]) for i, (a, b) in enumerate(zip(far, near))]
    for copy in copies:
        copy.start()
    for copy in copies:
        copy.wait()
    tokens, ids, weights = near
    tok_rows, features = tokens.shape
    half = features // 2
    for start in range(0, features, LANES):
        at = start % half // LANES * tok_rows
        outs[start // half][at : at + tok_rows] = tokens[:, start : start + LANES]
    place = lax.broadcasted_iota(jnp.int32, (num_experts, tok_rows), 0)
    share = jnp.zeros(place.shape, jnp.float32)
    for choice in range(ids.shape[0]):
        named = ids[choice : choice + 1] == place
        share += jnp.where(named, weights[choice : choice + 1], 0.0)
    high = share.astype(jnp.bfloat16).astype(jnp.float32)
    both = jnp.concatenate([high, share - high], axis=0)
    outs[1][half // LANES * tok_rows :] = both.astype(jnp.bfloat16)


def serve_rows(width, picks, partner, *refs):
    pieces, refs, out = refs[: -1 - 2 * len(picks)], refs[-1 - 2 * len(picks) : -1], refs[-1]
    tok_rows, _ = out.shape
    num_experts = len(partner)
    rows = [
        piece[at : at + tok_rows]
        for piece in pieces
        for at in range(0, piece.shape[0] - tok_rows + 1, tok_rows)
    ]
    rows = jnp.concatenate(rows, axis=1)
    shares = jnp.transpose(pieces[-1][-2 * num_experts :].astype(jnp.float32))
    lanes = lax.broadcasted_iota(jnp.int32, shares.shape, 1)
    me = lax.axis_index("expert")
    other = sum(jnp.where(me == e, partner[e], 0) for e in range(num_experts))
    total = None
    for place, which in enumerate(picks):
        gate, down = refs[2 * place], refs[2 * place + 1]
        expert = (me, other)[which]
        share = jnp.where((lanes == expert) | (lanes == expert + num_experts), shares, 0.0)
        share = jnp.sum(share, axis=1, keepdims=True)
        pre = jnp.dot(rows, gate[...], preferred_element_type=jnp.float32)
        gated, up = pre[:, :width], pre[:, width:]
        hidden = gated / (1.0 + jnp.exp(-gated)) * up * share
        part = lax.dot_general(
            hidden.astype(jnp.bfloat16),
            down[...],
            (((1,), (1,)), ((), ())),
            preferred_element_type=jnp.float32,
        )
        total = part if total is None else total + part
    out[...] = total


def ring(stops, tokens, expert_ids, route_weights, gate_up, down_t):
    tok_rows, features = tokens.shape
    num_experts, width = lax.axis_size("expert"), down_t.shape[2]
    count = len(stops)
    partner = [0] * num_experts
    onward = [0] * num_experts
    for s in range(count):
        for place, turn in ((0, 1), (1, -1)):
            partner[stops[s][place]] = stops[s][1 - place]
            onward[stops[s][place]] = stops[(s + turn) % count][place]
    hop = functools.partial(lax.ppermute, axis_name="expert", perm=list(enumerate(onward)))
    swap = functools.partial(lax.ppermute, axis_name="expert", perm=list(enumerate(partner)))
    whole = pl.BlockSpec(memory_space=pltpu.VMEM)

    given = (tokens, expert_ids.T, route_weights.T)
    given = [pltpu.with_memory_space_constraint(x, pltpu.HBM) for x in given]
    half = features // 2 // LANES * tok_rows
    packed = pl.pallas_call(
        functools.partial(pack_rows, num_experts),
        out_shape=[
            jax.ShapeDtypeStruct((rows, LANES), jnp.bfloat16)
            for rows in (half, half + 2 * num_experts)
        ],
        in_specs=[pl.BlockSpec(memory_space=pltpu.HBM)] * 3,
        out_specs=[whole] * 2,
        scratch_shapes=[pltpu.VMEM(x.shape, x.dtype) for x in given]
        + [pltpu.SemaphoreType.DMA((3,))],
        compiler_params=pltpu.CompilerParams(vmem_limit_bytes=8 * 1024 * 1024),
        name="pack_rows",
    )(*given)
    away = [hop(x) for x in packed]
    weights = [(gate_up[0], down_t[0])]
    weights.append(tuple(swap(w) for w in weights[0]))

    def serve(pieces, picks):
        return pl.pallas_call(
            functools.partial(serve_rows, width, picks, partner),
            out_shape=jax.ShapeDtypeStruct((tok_rows, features), jnp.float32),
            in_specs=[whole] * (len(pieces) + 2 * len(picks)),
            out_specs=whole,
            compiler_params=pltpu.CompilerParams(vmem_limit_bytes=8 * 1024 * 1024),
            name="serve_rows",
        )(*pieces, *(w for which in picks for w in weights[which]))

    def after(arrays, other):
        return [lax.optimization_barrier((x, other))[0] for x in arrays]

    home = serve(packed, (0,))
    away = after(away, home)
    total = None
    for step in range(1, count):
        here = away
        if step < count - 1:
            away = [hop(x) for x in (away if step == 1 else [jnp.concatenate(away)])]
        more = serve(here, (0, 1))
        away = after(away, more)
        parts = 2 if step >= count - 2 else 1
        more = jnp.split(more, parts)
        if total is not None:
            if len(total) < parts:
                total = jnp.split(total[0], parts)
        sent = []
        for at, x in enumerate(more):
            if total is not None:
                y = after([total[at]], sent)[0] if parts > 1 else total[at]
                x = x + y.astype(jnp.float32)
            sent.append(x.astype(jnp.bfloat16))
        total = []
        for x in sent:
            total.append(hop(x))
    home += serve(packed, (1,))
    return (home + jnp.concatenate(total).astype(jnp.float32)).astype(jnp.bfloat16)


def solution(mesh):
    placed = (
        P(("group", "expert", "token"), None),
        P(("group", "expert", "token"), None),
        P(("group", "expert", "token"), None),
        P("expert", "token", None),
        P("expert", "token", None),
    )

    stops = chip_cycle(mesh)
    cycle = mesh.shape["token"] == 1 and {len(s) for s in stops} == {2} and len(stops) > 2

    def per_device(tokens, expert_ids, route_weights, gate_up, down_t):
        fits = cycle and mesh.shape["expert"] <= 4 * expert_ids.shape[1] and gate_up.shape[0] == 1
        if fits and tokens.shape[0] == LANES and tokens.shape[1] % (2 * LANES) == 0:
            return ring(stops, tokens, expert_ids, route_weights, gate_up, down_t)
        return exchange_rows(tokens, expert_ids, route_weights, gate_up, down_t)

    return jax.shard_map(
        per_device,
        mesh=mesh,
        in_specs=placed,
        out_specs=P(("group", "expert", "token"), None),
        check_vma=False,
    )
```

```python
import functools

import jax
import jax.numpy as jnp
from jax import lax
from jax.experimental import pallas as pl
from jax.experimental.pallas import tpu as pltpu
from jax.sharding import PartitionSpec as P


def expert_apply(arrived, full_gate_up, full_down):
    shape = arrived.shape
    width = full_down.shape[2]
    rows = arrived.reshape(-1, shape[-1])
    pre = jnp.dot(rows, full_gate_up[0], preferred_element_type=jnp.float32)
    hidden = (jax.nn.silu(pre[:, :width]) * pre[:, width:]).astype(jnp.bfloat16)
    outputs = lax.dot_general(
        hidden, full_down[0], (((1,), (1,)), ((), ())), preferred_element_type=jnp.float32
    )
    return outputs.astype(jnp.bfloat16).reshape(shape)


def exchange_rows(tokens, expert_ids, route_weights, gate_up, down_t):
    tok_rows, choices_each = expert_ids.shape
    features = tokens.shape[1]
    num_experts = lax.axis_size("expert")
    slot_count = min(
        tok_rows, (3 * tok_rows * choices_each + 2 * num_experts - 1) // (2 * num_experts)
    )
    full_gate_up, full_down = (
        lax.all_gather(gate_up, "token", axis=1, tiled=True),
        lax.all_gather(down_t, "token", axis=1, tiled=True),
    )
    flat_ids = expert_ids.reshape(-1)
    onehot = (flat_ids[:, None] == jnp.arange(num_experts, dtype=jnp.int32)[None, :]).astype(
        jnp.int32
    )
    running = jnp.cumsum(onehot, axis=0)
    ranks = jnp.sum(running * onehot, axis=1) - 1
    slots = flat_ids * slot_count + ranks
    repeated = jnp.repeat(tokens, choices_each, axis=0)
    outgoing = jnp.zeros((num_experts * slot_count, features), jnp.bfloat16).at[slots].set(repeated)
    outgoing = outgoing.reshape(num_experts, slot_count, features)
    arrived = lax.all_to_all(outgoing, "expert", split_axis=0, concat_axis=0, tiled=True)
    served = expert_apply(arrived, full_gate_up, full_down)
    returned = lax.all_to_all(served, "expert", split_axis=0, concat_axis=0, tiled=True)
    picked = returned.reshape(num_experts * slot_count, features)[slots]
    picked = picked.reshape(tok_rows, choices_each, features)
    total = jnp.zeros((tok_rows, features), jnp.float32)
    for which in range(choices_each):
        total = total + route_weights[:, which : which + 1] * picked[:, which].astype(jnp.float32)
    return total.astype(jnp.bfloat16)


def chip_cycle(mesh):
    devices = mesh.devices[0, :, 0]
    chips = {}
    for index, device in enumerate(devices):
        chips.setdefault(tuple(getattr(device, "coords", (index // 2,))), []).append(index)
    coords = sorted(chips)
    wide = [d for d in range(len(coords[0])) if len({c[d] for c in coords}) > 1]
    if len(wide) == 2:
        wide.sort(key=lambda d: len({c[d] for c in coords}))
        short, long = wide
        turn = {v: i for i, v in enumerate(sorted({c[short] for c in coords}))}
        coords.sort(key=lambda c: (turn[c[short]], c[long] if turn[c[short]] % 2 == 0 else -c[long]))
    return [chips[c] for c in coords]


LANES = 128


def pack_rows(num_experts, *refs):
    far, outs, near, done = refs[:3], refs[3:5], refs[5:8], refs[8]
    copies = [pltpu.make_async_copy(a, b, done.at[i]) for i, (a, b) in enumerate(zip(far, near))]
    for copy in copies:
        copy.start()
    for copy in copies:
        copy.wait()
    tokens, ids, weights = near
    tok_rows, features = tokens.shape
    half = features // 2
    for start in range(0, features, LANES):
        at = start % half // LANES * tok_rows
        outs[start // half][at : at + tok_rows] = tokens[:, start : start + LANES]
    place = lax.broadcasted_iota(jnp.int32, (num_experts, tok_rows), 0)
    share = jnp.zeros(place.shape, jnp.float32)
    for choice in range(ids.shape[0]):
        named = ids[choice : choice + 1] == place
        share += jnp.where(named, weights[choice : choice + 1], 0.0)
    high = share.astype(jnp.bfloat16).astype(jnp.float32)
    both = jnp.concatenate([high, share - high], axis=0)
    outs[1][half // LANES * tok_rows :] = both.astype(jnp.bfloat16)


def load(*refs):
    count = len(refs) // 2
    done = refs[-1]
    copies = [pltpu.make_async_copy(refs[i], refs[count + i], done.at[i]) for i in range(count)]
    for copy in copies:
        copy.start()
    for copy in copies:
        copy.wait()


def serve_rows(width, picks, partner, *refs):
    pieces, refs, out = refs[: -1 - 2 * len(picks)], refs[-1 - 2 * len(picks) : -1], refs[-1]
    tok_rows, _ = out.shape
    num_experts = len(partner)
    rows = [
        piece[at : at + tok_rows]
        for piece in pieces
        for at in range(0, piece.shape[0] - tok_rows + 1, tok_rows)
    ]
    rows = jnp.concatenate(rows, axis=1)
    shares = jnp.transpose(pieces[-1][-2 * num_experts :].astype(jnp.float32))
    lanes = lax.broadcasted_iota(jnp.int32, shares.shape, 1)
    me = lax.axis_index("expert")
    other = sum(jnp.where(me == e, partner[e], 0) for e in range(num_experts))
    total = None
    for place, which in enumerate(picks):
        gate, down = refs[2 * place], refs[2 * place + 1]
        expert = (me, other)[which]
        share = jnp.where((lanes == expert) | (lanes == expert + num_experts), shares, 0.0)
        share = jnp.sum(share, axis=1, keepdims=True)
        pre = jnp.dot(rows, gate[...], preferred_element_type=jnp.float32)
        gated, up = pre[:, :width], pre[:, width:]
        hidden = gated / (1.0 + jnp.exp(-gated)) * up * share
        part = lax.dot_general(
            hidden.astype(jnp.bfloat16),
            down[...],
            (((1,), (1,)), ((), ())),
            preferred_element_type=jnp.float32,
        )
        total = part if total is None else total + part
    out[...] = total


def ring(stops, tokens, expert_ids, route_weights, gate_up, down_t):
    tok_rows, features = tokens.shape
    num_experts, width = lax.axis_size("expert"), down_t.shape[2]
    count = len(stops)
    partner = [0] * num_experts
    onward = [0] * num_experts
    for s in range(count):
        for place, turn in ((0, 1), (1, -1)):
            partner[stops[s][place]] = stops[s][1 - place]
            onward[stops[s][place]] = stops[(s + turn) % count][place]
    hop = functools.partial(lax.ppermute, axis_name="expert", perm=list(enumerate(onward)))
    swap = functools.partial(lax.ppermute, axis_name="expert", perm=list(enumerate(partner)))
    whole = pl.BlockSpec(memory_space=pltpu.VMEM)

    given = (tokens, expert_ids.T, route_weights.T)
    given = [pltpu.with_memory_space_constraint(x, pltpu.HBM) for x in given]
    half = features // 2 // LANES * tok_rows
    packed = pl.pallas_call(
        functools.partial(pack_rows, num_experts),
        out_shape=[
            jax.ShapeDtypeStruct((rows, LANES), jnp.bfloat16)
            for rows in (half, half + 2 * num_experts)
        ],
        in_specs=[pl.BlockSpec(memory_space=pltpu.HBM)] * 3,
        out_specs=[whole] * 2,
        scratch_shapes=[pltpu.VMEM(x.shape, x.dtype) for x in given]
        + [pltpu.SemaphoreType.DMA((3,))],
        compiler_params=pltpu.CompilerParams(vmem_limit_bytes=8 * 1024 * 1024),
        name="pack_rows",
    )(*given)
    away = [hop(x) for x in packed]
    own = (gate_up[0], down_t[0])
    swapped = [swap(w) for w in own]
    held = pl.pallas_call(
        load,
        out_shape=[jax.ShapeDtypeStruct(w.shape, w.dtype) for w in own],
        in_specs=[pl.BlockSpec(memory_space=pltpu.HBM)] * 2,
        out_specs=[whole] * 2,
        scratch_shapes=[pltpu.SemaphoreType.DMA((2,))],
        compiler_params=pltpu.CompilerParams(vmem_limit_bytes=2 * 1024 * 1024),
        name="load",
    )(*(pltpu.with_memory_space_constraint(w, pltpu.HBM) for w in own))
    weights = (held, swapped)

    def serve(pieces, picks):
        return pl.pallas_call(
            functools.partial(serve_rows, width, picks, partner),
            out_shape=jax.ShapeDtypeStruct((tok_rows, features), jnp.float32),
            in_specs=[whole] * (len(pieces) + 2 * len(picks)),
            out_specs=whole,
            compiler_params=pltpu.CompilerParams(vmem_limit_bytes=8 * 1024 * 1024),
            name="serve_rows",
        )(*pieces, *(w for which in picks for w in weights[which]))

    def after(arrays, other):
        return [lax.optimization_barrier((x, other))[0] for x in arrays]

    away = after(away, held)
    total = None
    for step in range(1, count):
        here = list(away)
        if step < count - 1:
            away = away if step == 1 else [jnp.concatenate(away)]
            for at, x in enumerate(away):
                away[at] = hop(x)
        more = serve(here, (0, 1))
        away = after(away, more)
        parts = 2 if step >= count - 2 else 1
        more = jnp.split(more, parts)
        if total is not None:
            if len(total) < parts:
                total = jnp.split(total[0], parts)
        sent = []
        for at, x in enumerate(more):
            if total is not None:
                y = after([total[at]], sent)[0] if parts > 1 else total[at]
                x = x + y.astype(jnp.float32)
            sent.append(x.astype(jnp.bfloat16))
        total = []
        for x in sent:
            total.append(hop(x))
    home = serve(packed, (0, 1))
    return (home + jnp.concatenate(total).astype(jnp.float32)).astype(jnp.bfloat16)


def solution(mesh):
    placed = (
        P(("group", "expert", "token"), None),
        P(("group", "expert", "token"), None),
        P(("group", "expert", "token"), None),
        P("expert", "token", None),
        P("expert", "token", None),
    )

    stops = chip_cycle(mesh)
    cycle = mesh.shape["token"] == 1 and {len(s) for s in stops} == {2} and len(stops) > 2

    def per_device(tokens, expert_ids, route_weights, gate_up, down_t):
        fits = cycle and mesh.shape["expert"] <= 4 * expert_ids.shape[1] and gate_up.shape[0] == 1
        if fits and tokens.shape[0] == LANES and tokens.shape[1] % (2 * LANES) == 0:
            return ring(stops, tokens, expert_ids, route_weights, gate_up, down_t)
        return exchange_rows(tokens, expert_ids, route_weights, gate_up, down_t)

    return jax.shard_map(
        per_device,
        mesh=mesh,
        in_specs=placed,
        out_specs=P(("group", "expert", "token"), None),
        check_vma=False,
    )
```

```python
import functools

import jax
import jax.numpy as jnp
from jax import lax
from jax.experimental import pallas as pl
from jax.experimental.pallas import tpu as pltpu
from jax.sharding import PartitionSpec as P


def expert_apply(arrived, full_gate_up, full_down):
    shape = arrived.shape
    width = full_down.shape[2]
    rows = arrived.reshape(-1, shape[-1])
    pre = jnp.dot(rows, full_gate_up[0], preferred_element_type=jnp.float32)
    hidden = (jax.nn.silu(pre[:, :width]) * pre[:, width:]).astype(jnp.bfloat16)
    outputs = lax.dot_general(
        hidden, full_down[0], (((1,), (1,)), ((), ())), preferred_element_type=jnp.float32
    )
    return outputs.astype(jnp.bfloat16).reshape(shape)


def exchange_rows(tokens, expert_ids, route_weights, gate_up, down_t):
    tok_rows, choices_each = expert_ids.shape
    features = tokens.shape[1]
    num_experts = lax.axis_size("expert")
    slot_count = min(
        tok_rows, (3 * tok_rows * choices_each + 2 * num_experts - 1) // (2 * num_experts)
    )
    full_gate_up, full_down = (
        lax.all_gather(gate_up, "token", axis=1, tiled=True),
        lax.all_gather(down_t, "token", axis=1, tiled=True),
    )
    flat_ids = expert_ids.reshape(-1)
    onehot = (flat_ids[:, None] == jnp.arange(num_experts, dtype=jnp.int32)[None, :]).astype(
        jnp.int32
    )
    running = jnp.cumsum(onehot, axis=0)
    ranks = jnp.sum(running * onehot, axis=1) - 1
    slots = flat_ids * slot_count + ranks
    repeated = jnp.repeat(tokens, choices_each, axis=0)
    outgoing = jnp.zeros((num_experts * slot_count, features), jnp.bfloat16).at[slots].set(repeated)
    outgoing = outgoing.reshape(num_experts, slot_count, features)
    arrived = lax.all_to_all(outgoing, "expert", split_axis=0, concat_axis=0, tiled=True)
    served = expert_apply(arrived, full_gate_up, full_down)
    returned = lax.all_to_all(served, "expert", split_axis=0, concat_axis=0, tiled=True)
    picked = returned.reshape(num_experts * slot_count, features)[slots]
    picked = picked.reshape(tok_rows, choices_each, features)
    total = jnp.zeros((tok_rows, features), jnp.float32)
    for which in range(choices_each):
        total = total + route_weights[:, which : which + 1] * picked[:, which].astype(jnp.float32)
    return total.astype(jnp.bfloat16)


def chip_cycle(mesh):
    devices = mesh.devices[0, :, 0]
    chips = {}
    for index, device in enumerate(devices):
        chips.setdefault(tuple(getattr(device, "coords", (index // 2,))), []).append(index)
    coords = sorted(chips)
    wide = [d for d in range(len(coords[0])) if len({c[d] for c in coords}) > 1]
    if len(wide) == 2:
        wide.sort(key=lambda d: len({c[d] for c in coords}))
        short, long = wide
        turn = {v: i for i, v in enumerate(sorted({c[short] for c in coords}))}
        coords.sort(key=lambda c: (turn[c[short]], c[long] if turn[c[short]] % 2 == 0 else -c[long]))
    return [chips[c] for c in coords]


LANES = 128


def pack_rows(num_experts, tokens, ids_far, weights_far, out_a, out_b, ids, weights, done):
    outs = (out_a, out_b)
    tok_rows, features = tokens.shape
    half = features // 2
    pairs = [(ids_far, ids), (weights_far, weights)]
    for start in range(0, features, LANES):
        at = start % half // LANES * tok_rows
        pairs.append(
            (tokens.at[:, start : start + LANES], outs[start // half].at[at : at + tok_rows])
        )
    copies = [pltpu.make_async_copy(a, b, done.at[i]) for i, (a, b) in enumerate(pairs)]
    for copy in copies:
        copy.start()
    for copy in copies[:2]:
        copy.wait()
    place = lax.broadcasted_iota(jnp.int32, (num_experts, tok_rows), 0)
    share = jnp.zeros(place.shape, jnp.float32)
    for choice in range(ids.shape[0]):
        named = ids[choice : choice + 1] == place
        share += jnp.where(named, weights[choice : choice + 1], 0.0)
    high = share.astype(jnp.bfloat16).astype(jnp.float32)
    both = jnp.concatenate([high, share - high], axis=0)
    out_b[half // LANES * tok_rows :] = both.astype(jnp.bfloat16)
    for copy in copies[2:]:
        copy.wait()


def load(*refs):
    count = len(refs) // 2
    done = refs[-1]
    copies = [pltpu.make_async_copy(refs[i], refs[count + i], done.at[i]) for i in range(count)]
    for copy in copies:
        copy.start()
    for copy in copies:
        copy.wait()


def serve_rows(width, picks, partner, *refs):
    pieces, refs, out = refs[: -1 - 2 * len(picks)], refs[-1 - 2 * len(picks) : -1], refs[-1]
    tok_rows, _ = out.shape
    num_experts = len(partner)
    rows = [
        piece[at : at + tok_rows]
        for piece in pieces
        for at in range(0, piece.shape[0] - tok_rows + 1, tok_rows)
    ]
    rows = jnp.concatenate(rows, axis=1)
    shares = jnp.transpose(pieces[-1][-2 * num_experts :].astype(jnp.float32))
    lanes = lax.broadcasted_iota(jnp.int32, shares.shape, 1)
    me = lax.axis_index("expert")
    other = sum(jnp.where(me == e, partner[e], 0) for e in range(num_experts))
    total = None
    for place, which in enumerate(picks):
        gate, down = refs[2 * place], refs[2 * place + 1]
        expert = (me, other)[which]
        share = jnp.where((lanes == expert) | (lanes == expert + num_experts), shares, 0.0)
        share = jnp.sum(share, axis=1, keepdims=True)
        pre = jnp.dot(rows, gate[...], preferred_element_type=jnp.float32)
        gated, up = pre[:, :width], pre[:, width:]
        hidden = gated / (1.0 + jnp.exp(-gated)) * up
        part = lax.dot_general(
            hidden.astype(jnp.bfloat16),
            down[...],
            (((1,), (1,)), ((), ())),
            preferred_element_type=jnp.float32,
        )
        part = share * part.astype(jnp.bfloat16).astype(jnp.float32)
        total = part if total is None else total + part
    out[...] = total


def finish(at, home, got, *refs):
    out, rows, done = refs[-3:]
    count = got.shape[0]
    rows[...] = (home[at : at + count] + got[...].astype(jnp.float32)).astype(rows.dtype)
    copy = pltpu.make_async_copy(rows, out.at[at : at + count], done)
    copy.start()
    copy.wait()


def ring(stops, tokens, expert_ids, route_weights, gate_up, down_t):
    tok_rows, features = tokens.shape
    num_experts, width = lax.axis_size("expert"), down_t.shape[2]
    count = len(stops)
    partner = [0] * num_experts
    onward = [0] * num_experts
    for s in range(count):
        for place, turn in ((0, 1), (1, -1)):
            partner[stops[s][place]] = stops[s][1 - place]
            onward[stops[s][place]] = stops[(s + turn) % count][place]
    hop = functools.partial(lax.ppermute, axis_name="expert", perm=list(enumerate(onward)))
    swap = functools.partial(lax.ppermute, axis_name="expert", perm=list(enumerate(partner)))
    whole = pl.BlockSpec(memory_space=pltpu.VMEM)

    given = (tokens, expert_ids.T, route_weights.T)
    given = [pltpu.with_memory_space_constraint(x, pltpu.HBM) for x in given]
    half = features // 2 // LANES * tok_rows
    packed = pl.pallas_call(
        functools.partial(pack_rows, num_experts),
        out_shape=[
            jax.ShapeDtypeStruct((rows, LANES), jnp.bfloat16)
            for rows in (half, half + 2 * num_experts)
        ],
        in_specs=[pl.BlockSpec(memory_space=pltpu.HBM)] * 3,
        out_specs=[whole] * 2,
        scratch_shapes=[pltpu.VMEM(x.shape, x.dtype) for x in given[1:]]
        + [pltpu.SemaphoreType.DMA((2 + features // LANES,))],
        compiler_params=pltpu.CompilerParams(vmem_limit_bytes=8 * 1024 * 1024),
        name="pack_rows",
    )(*given)
    away = []
    for x in packed:
        away.append(hop(x))
    own = (gate_up[0], down_t[0])
    swapped = [swap(w) for w in own]
    held = pl.pallas_call(
        load,
        out_shape=[jax.ShapeDtypeStruct(w.shape, w.dtype) for w in own],
        in_specs=[pl.BlockSpec(memory_space=pltpu.HBM)] * 2,
        out_specs=[whole] * 2,
        scratch_shapes=[pltpu.SemaphoreType.DMA((2,))],
        compiler_params=pltpu.CompilerParams(vmem_limit_bytes=2 * 1024 * 1024),
        name="load",
    )(*(pltpu.with_memory_space_constraint(w, pltpu.HBM) for w in own))
    weights = (held, swapped)

    def serve(pieces, picks):
        return pl.pallas_call(
            functools.partial(serve_rows, width, picks, partner),
            out_shape=jax.ShapeDtypeStruct((tok_rows, features), jnp.float32),
            in_specs=[whole] * (len(pieces) + 2 * len(picks)),
            out_specs=whole,
            compiler_params=pltpu.CompilerParams(vmem_limit_bytes=8 * 1024 * 1024),
            name="serve_rows",
        )(*pieces, *(w for which in picks for w in weights[which]))

    def after(arrays, other):
        return [lax.optimization_barrier((x, other))[0] for x in arrays]

    away = after(away, held)
    total = None
    for step in range(1, count):
        here = list(away)
        if step < count - 1:
            away = away if step == 1 else [jnp.concatenate(away)]
            for at, x in enumerate(away):
                away[at] = hop(x)
        more = serve(here, (0, 1))
        away = after(away, more)
        parts = 2 if step >= count - 2 else 1
        more = jnp.split(more, parts)
        if total is not None:
            if len(total) < parts:
                total = jnp.split(total[0], parts)
        sent = []
        for at, x in enumerate(more):
            if total is not None:
                y = after([total[at]], sent)[0] if parts > 1 else total[at]
                x = x + y.astype(jnp.float32)
            sent.append(x.astype(jnp.bfloat16))
        total = []
        for x in sent:
            total.append(hop(x))
    home = serve(packed, (0, 1))
    far = pl.BlockSpec(memory_space=pltpu.HBM)
    out, rows = [], tok_rows // len(total)
    for at, got in enumerate(total):
        out = [
            pl.pallas_call(
                functools.partial(finish, at * rows),
                out_shape=jax.ShapeDtypeStruct(tokens.shape, tokens.dtype),
                in_specs=[whole] * 2 + [far] * len(out),
                out_specs=far,
                input_output_aliases={2: 0} if out else {},
                scratch_shapes=[
                    pltpu.VMEM((rows, features), tokens.dtype),
                    pltpu.SemaphoreType.DMA(()),
                ],
                compiler_params=pltpu.CompilerParams(vmem_limit_bytes=4 * 1024 * 1024),
                name="finish",
            )(home, got, *out)
        ]
    return out[0]


def solution(mesh):
    placed = (
        P(("group", "expert", "token"), None),
        P(("group", "expert", "token"), None),
        P(("group", "expert", "token"), None),
        P("expert", "token", None),
        P("expert", "token", None),
    )

    stops = chip_cycle(mesh)
    cycle = mesh.shape["token"] == 1 and {len(s) for s in stops} == {2} and len(stops) > 2

    def per_device(tokens, expert_ids, route_weights, gate_up, down_t):
        fits = cycle and mesh.shape["expert"] <= 4 * expert_ids.shape[1] and gate_up.shape[0] == 1
        if fits and tokens.shape[0] == LANES and tokens.shape[1] % (2 * LANES) == 0:
            return ring(stops, tokens, expert_ids, route_weights, gate_up, down_t)
        return exchange_rows(tokens, expert_ids, route_weights, gate_up, down_t)

    return jax.shard_map(
        per_device,
        mesh=mesh,
        in_specs=placed,
        out_specs=P(("group", "expert", "token"), None),
        check_vma=False,
    )
```

```python
import functools

import jax
import jax.numpy as jnp
from jax import lax
from jax.experimental import pallas as pl
from jax.experimental.pallas import tpu as pltpu
from jax.sharding import PartitionSpec as P


def expert_apply(arrived, full_gate_up, full_down):
    shape = arrived.shape
    width = full_down.shape[2]
    rows = arrived.reshape(-1, shape[-1])
    pre = jnp.dot(rows, full_gate_up[0], preferred_element_type=jnp.float32)
    hidden = (jax.nn.silu(pre[:, :width]) * pre[:, width:]).astype(jnp.bfloat16)
    outputs = lax.dot_general(
        hidden, full_down[0], (((1,), (1,)), ((), ())), preferred_element_type=jnp.float32
    )
    return outputs.astype(jnp.bfloat16).reshape(shape)


def exchange_rows(tokens, expert_ids, route_weights, gate_up, down_t):
    tok_rows, choices_each = expert_ids.shape
    features = tokens.shape[1]
    num_experts = lax.axis_size("expert")
    slot_count = min(
        tok_rows, (3 * tok_rows * choices_each + 2 * num_experts - 1) // (2 * num_experts)
    )
    full_gate_up, full_down = (
        lax.all_gather(gate_up, "token", axis=1, tiled=True),
        lax.all_gather(down_t, "token", axis=1, tiled=True),
    )
    flat_ids = expert_ids.reshape(-1)
    onehot = (flat_ids[:, None] == jnp.arange(num_experts, dtype=jnp.int32)[None, :]).astype(
        jnp.int32
    )
    running = jnp.cumsum(onehot, axis=0)
    ranks = jnp.sum(running * onehot, axis=1) - 1
    slots = flat_ids * slot_count + ranks
    repeated = jnp.repeat(tokens, choices_each, axis=0)
    outgoing = jnp.zeros((num_experts * slot_count, features), jnp.bfloat16).at[slots].set(repeated)
    outgoing = outgoing.reshape(num_experts, slot_count, features)
    arrived = lax.all_to_all(outgoing, "expert", split_axis=0, concat_axis=0, tiled=True)
    served = expert_apply(arrived, full_gate_up, full_down)
    returned = lax.all_to_all(served, "expert", split_axis=0, concat_axis=0, tiled=True)
    picked = returned.reshape(num_experts * slot_count, features)[slots]
    picked = picked.reshape(tok_rows, choices_each, features)
    total = jnp.zeros((tok_rows, features), jnp.float32)
    for which in range(choices_each):
        total = total + route_weights[:, which : which + 1] * picked[:, which].astype(jnp.float32)
    return total.astype(jnp.bfloat16)


def chip_cycle(mesh):
    devices = mesh.devices[0, :, 0]
    chips = {}
    for index, device in enumerate(devices):
        chips.setdefault(tuple(getattr(device, "coords", (index // 2,))), []).append(index)
    coords = sorted(chips)
    wide = [d for d in range(len(coords[0])) if len({c[d] for c in coords}) > 1]
    if len(wide) == 2:
        wide.sort(key=lambda d: len({c[d] for c in coords}))
        short, long = wide
        turn = {v: i for i, v in enumerate(sorted({c[short] for c in coords}))}
        coords.sort(key=lambda c: (turn[c[short]], c[long] if turn[c[short]] % 2 == 0 else -c[long]))
    return [chips[c] for c in coords]


LANES = 128


def start_copies(pairs, done):
    copies = [pltpu.make_async_copy(a, b, done.at[i]) for i, (a, b) in enumerate(pairs)]
    for copy in copies:
        copy.start()
    return copies


def column_blocks(tokens, start, out):
    tok_rows = tokens.shape[0]
    for at in range(0, out.shape[0] - tok_rows + 1, tok_rows):
        lane = start + at // tok_rows * LANES
        yield tokens.at[:, lane : lane + LANES], out.at[at : at + tok_rows]


def pack_rows(tokens, out, done):
    for copy in start_copies(column_blocks(tokens, 0, out), done):
        copy.wait()


def pack_shares(num_experts, tokens, ids_far, weights_far, out, ids, weights, done):
    tok_rows, features = tokens.shape
    pairs = [(ids_far, ids), (weights_far, weights)]
    copies = start_copies([*pairs, *column_blocks(tokens, features // 2, out)], done)
    for copy in copies[:2]:
        copy.wait()
    place = lax.broadcasted_iota(jnp.int32, (num_experts, tok_rows), 0)
    share = jnp.zeros(place.shape, jnp.float32)
    for choice in range(ids.shape[0]):
        named = ids[choice : choice + 1] == place
        share += jnp.where(named, weights[choice : choice + 1], 0.0)
    high = share.astype(jnp.bfloat16).astype(jnp.float32)
    both = jnp.concatenate([high, share - high], axis=0)
    out[-2 * num_experts :] = both.astype(jnp.bfloat16)
    for copy in copies[2:]:
        copy.wait()


def load(*refs):
    count = len(refs) // 2
    for copy in start_copies(zip(refs[:count], refs[count : 2 * count]), refs[-1]):
        copy.wait()


def serve_rows(width, tok_rows, first, partner, *refs):
    pieces, refs, out = refs[:-5], refs[-5:-1], refs[-1]
    last = first + out.shape[0]
    num_experts = len(partner)
    rows = [
        piece[at + first : at + last]
        for piece in pieces
        for at in range(0, piece.shape[0] - tok_rows + 1, tok_rows)
    ]
    rows = jnp.concatenate(rows, axis=1)
    shares = jnp.transpose(pieces[-1][-2 * num_experts :].astype(jnp.float32))[first:last]
    lanes = lax.broadcasted_iota(jnp.int32, shares.shape, 1)
    me = lax.axis_index("expert")
    other = sum(jnp.where(me == e, partner[e], 0) for e in range(num_experts))
    total = None
    for expert, gate, down in ((me, *refs[:2]), (other, *refs[2:])):
        share = jnp.where((lanes == expert) | (lanes == expert + num_experts), shares, 0.0)
        share = jnp.sum(share, axis=1, keepdims=True)
        pre = jnp.dot(rows, gate[...], preferred_element_type=jnp.float32)
        gated, up = pre[:, :width], pre[:, width:]
        hidden = gated / (1.0 + jnp.exp(-gated)) * up
        part = lax.dot_general(
            hidden.astype(jnp.bfloat16),
            down[...],
            (((1,), (1,)), ((), ())),
            preferred_element_type=jnp.float32,
        )
        part = share * part.astype(jnp.bfloat16).astype(jnp.float32)
        total = part if total is None else total + part
    out[...] = total


def finish(at, home, got, *refs):
    out, rows, done = refs[-3:]
    count = got.shape[0]
    rows[...] = (home[at : at + count] + got[...].astype(jnp.float32)).astype(rows.dtype)
    copy = pltpu.make_async_copy(rows, out.at[at : at + count], done)
    copy.start()
    copy.wait()


def ring(stops, tokens, expert_ids, route_weights, gate_up, down_t):
    tok_rows, features = tokens.shape
    num_experts, width = lax.axis_size("expert"), down_t.shape[2]
    count = len(stops)
    partner = [0] * num_experts
    onward = [0] * num_experts
    for s in range(count):
        for place, turn in ((0, 1), (1, -1)):
            partner[stops[s][place]] = stops[s][1 - place]
            onward[stops[s][place]] = stops[(s + turn) % count][place]
    hop = functools.partial(lax.ppermute, axis_name="expert", perm=list(enumerate(onward)))
    swap = functools.partial(lax.ppermute, axis_name="expert", perm=list(enumerate(partner)))
    whole = pl.BlockSpec(memory_space=pltpu.VMEM)

    far = pl.BlockSpec(memory_space=pltpu.HBM)
    given = (tokens, expert_ids.T, route_weights.T)
    given = [pltpu.with_memory_space_constraint(x, pltpu.HBM) for x in given]
    half = features // 2 // LANES * tok_rows
    blocks = half // tok_rows
    small = pltpu.CompilerParams(vmem_limit_bytes=4 * 1024 * 1024)
    packed = [
        pl.pallas_call(
            pack_rows,
            out_shape=jax.ShapeDtypeStruct((half, LANES), jnp.bfloat16),
            in_specs=[far],
            out_specs=whole,
            scratch_shapes=[pltpu.SemaphoreType.DMA((blocks,))],
            compiler_params=small,
            name="pack_rows",
        )(given[0])
    ]
    packed.append(
        pl.pallas_call(
            functools.partial(pack_shares, num_experts),
            out_shape=jax.ShapeDtypeStruct((half + 2 * num_experts, LANES), jnp.bfloat16),
            in_specs=[far] * 3,
            out_specs=whole,
            scratch_shapes=[pltpu.VMEM(x.shape, x.dtype) for x in given[1:]]
            + [pltpu.SemaphoreType.DMA((2 + blocks,))],
            compiler_params=small,
            name="pack_shares",
        )(*given)
    )
    away = []
    for x in packed:
        away.append(hop(x))
    own = (gate_up[0], down_t[0])
    swapped = [swap(w) for w in own]
    held = pl.pallas_call(
        load,
        out_shape=[jax.ShapeDtypeStruct(w.shape, w.dtype) for w in own],
        in_specs=[pl.BlockSpec(memory_space=pltpu.HBM)] * 2,
        out_specs=[whole] * 2,
        scratch_shapes=[pltpu.SemaphoreType.DMA((2,))],
        compiler_params=pltpu.CompilerParams(vmem_limit_bytes=2 * 1024 * 1024),
        name="load",
    )(*(pltpu.with_memory_space_constraint(w, pltpu.HBM) for w in own))
    weights = (*held, *swapped)

    def serve(pieces, first, rows):
        return pl.pallas_call(
            functools.partial(serve_rows, width, tok_rows, first, partner),
            out_shape=jax.ShapeDtypeStruct((rows, features), jnp.float32),
            in_specs=[whole] * (len(pieces) + len(weights)),
            out_specs=whole,
            compiler_params=pltpu.CompilerParams(vmem_limit_bytes=8 * 1024 * 1024),
            name="serve_rows",
        )(*pieces, *weights)

    def after(arrays, other):
        return [lax.optimization_barrier((x, other))[0] for x in arrays]

    away = after(away, held)
    total = None
    for step in range(1, count):
        here = list(away)
        if step < count - 1:
            away = away if step == 1 else [jnp.concatenate(away)]
            for at, x in enumerate(away):
                away[at] = hop(x)
        parts = 2 if step == 1 or step >= count - 2 else 1
        if step == 1:
            more = []
            for at in range(parts):
                more.append(serve(here, at * tok_rows // parts, tok_rows // parts))
            away = after(away, tuple(more))
        else:
            more = serve(here, 0, tok_rows)
            away = after(away, more)
            more = jnp.split(more, parts)
        if total is not None and len(total) != parts:
            total = jnp.split(total[0], parts) if len(total) < parts else [jnp.concatenate(total)]
        sent = []
        for at, x in enumerate(more):
            if total is not None:
                y = after([total[at]], sent)[0] if parts > 1 else total[at]
                x = x + y.astype(jnp.float32)
            sent.append(x.astype(jnp.bfloat16))
        total = []
        for x in sent:
            total.append(hop(x))
    home = serve(packed, 0, tok_rows)
    out, rows = [], tok_rows // len(total)
    for at, got in enumerate(total):
        out = [
            pl.pallas_call(
                functools.partial(finish, at * rows),
                out_shape=jax.ShapeDtypeStruct(tokens.shape, tokens.dtype),
                in_specs=[whole] * 2 + [far] * len(out),
                out_specs=far,
                input_output_aliases={2: 0} if out else {},
                scratch_shapes=[
                    pltpu.VMEM((rows, features), tokens.dtype),
                    pltpu.SemaphoreType.DMA(()),
                ],
                compiler_params=small,
                name="finish",
            )(home, got, *out)
        ]
    return out[0]


def solution(mesh):
    placed = (
        P(("group", "expert", "token"), None),
        P(("group", "expert", "token"), None),
        P(("group", "expert", "token"), None),
        P("expert", "token", None),
        P("expert", "token", None),
    )

    stops = chip_cycle(mesh)
    cycle = mesh.shape["token"] == 1 and {len(s) for s in stops} == {2} and len(stops) > 4

    def per_device(tokens, expert_ids, route_weights, gate_up, down_t):
        fits = cycle and mesh.shape["expert"] <= 4 * expert_ids.shape[1] and gate_up.shape[0] == 1
        if fits and tokens.shape[0] == LANES and tokens.shape[1] % (2 * LANES) == 0:
            return ring(stops, tokens, expert_ids, route_weights, gate_up, down_t)
        return exchange_rows(tokens, expert_ids, route_weights, gate_up, down_t)

    return jax.shard_map(
        per_device,
        mesh=mesh,
        in_specs=placed,
        out_specs=P(("group", "expert", "token"), None),
        check_vma=False,
    )
```

```python
import functools

import jax
import jax.numpy as jnp
from jax import lax
from jax.experimental import pallas as pl
from jax.experimental.pallas import tpu as pltpu
from jax.sharding import PartitionSpec as P


def expert_apply(arrived, full_gate_up, full_down):
    shape = arrived.shape
    width = full_down.shape[2]
    rows = arrived.reshape(-1, shape[-1])
    pre = jnp.dot(rows, full_gate_up[0], preferred_element_type=jnp.float32)
    hidden = (jax.nn.silu(pre[:, :width]) * pre[:, width:]).astype(jnp.bfloat16)
    outputs = lax.dot_general(
        hidden, full_down[0], (((1,), (1,)), ((), ())), preferred_element_type=jnp.float32
    )
    return outputs.astype(jnp.bfloat16).reshape(shape)


def exchange_rows(tokens, expert_ids, route_weights, gate_up, down_t):
    tok_rows, choices_each = expert_ids.shape
    features = tokens.shape[1]
    num_experts = lax.axis_size("expert")
    slot_count = min(
        tok_rows, (3 * tok_rows * choices_each + 2 * num_experts - 1) // (2 * num_experts)
    )
    full_gate_up, full_down = (
        lax.all_gather(gate_up, "token", axis=1, tiled=True),
        lax.all_gather(down_t, "token", axis=1, tiled=True),
    )
    flat_ids = expert_ids.reshape(-1)
    onehot = (flat_ids[:, None] == jnp.arange(num_experts, dtype=jnp.int32)[None, :]).astype(
        jnp.int32
    )
    running = jnp.cumsum(onehot, axis=0)
    ranks = jnp.sum(running * onehot, axis=1) - 1
    slots = flat_ids * slot_count + ranks
    repeated = jnp.repeat(tokens, choices_each, axis=0)
    outgoing = jnp.zeros((num_experts * slot_count, features), jnp.bfloat16).at[slots].set(repeated)
    outgoing = outgoing.reshape(num_experts, slot_count, features)
    arrived = lax.all_to_all(outgoing, "expert", split_axis=0, concat_axis=0, tiled=True)
    served = expert_apply(arrived, full_gate_up, full_down)
    returned = lax.all_to_all(served, "expert", split_axis=0, concat_axis=0, tiled=True)
    picked = returned.reshape(num_experts * slot_count, features)[slots]
    picked = picked.reshape(tok_rows, choices_each, features)
    total = jnp.zeros((tok_rows, features), jnp.float32)
    for which in range(choices_each):
        total = total + route_weights[:, which : which + 1] * picked[:, which].astype(jnp.float32)
    return total.astype(jnp.bfloat16)


def chip_cycle(mesh):
    devices = mesh.devices[0, :, 0]
    chips = {}
    for index, device in enumerate(devices):
        chips.setdefault(tuple(getattr(device, "coords", (index // 2,))), []).append(index)
    coords = sorted(chips)
    wide = [d for d in range(len(coords[0])) if len({c[d] for c in coords}) > 1]
    if len(wide) == 2:
        wide.sort(key=lambda d: len({c[d] for c in coords}))
        short, long = wide
        turn = {v: i for i, v in enumerate(sorted({c[short] for c in coords}))}
        coords.sort(key=lambda c: (turn[c[short]], c[long] if turn[c[short]] % 2 == 0 else -c[long]))
    return [chips[c] for c in coords]


LANES = 128


def pack_rows(num_experts, tokens, ids_far, weights_far, out_a, out_b, ids, weights, done):
    outs = (out_a, out_b)
    tok_rows, features = tokens.shape
    half = features // 2
    pairs = [(ids_far, ids), (weights_far, weights)]
    for start in range(0, features, LANES):
        at = start % half // LANES * tok_rows
        pairs.append(
            (tokens.at[:, start : start + LANES], outs[start // half].at[at : at + tok_rows])
        )
    copies = [pltpu.make_async_copy(a, b, done.at[i]) for i, (a, b) in enumerate(pairs)]
    for copy in copies:
        copy.start()
    for copy in copies[:2]:
        copy.wait()
    place = lax.broadcasted_iota(jnp.int32, (num_experts, tok_rows), 0)
    share = jnp.zeros(place.shape, jnp.float32)
    for choice in range(ids.shape[0]):
        named = ids[choice : choice + 1] == place
        share += jnp.where(named, weights[choice : choice + 1], 0.0)
    high = share.astype(jnp.bfloat16).astype(jnp.float32)
    both = jnp.concatenate([high, share - high], axis=0)
    out_b[half // LANES * tok_rows :] = both.astype(jnp.bfloat16)
    for copy in copies[2:]:
        copy.wait()


def load(*refs):
    count = len(refs) // 2
    done = refs[-1]
    copies = [pltpu.make_async_copy(refs[i], refs[count + i], done.at[i]) for i in range(count)]
    for copy in copies:
        copy.start()
    for copy in copies:
        copy.wait()


def serve_rows(width, picks, partner, *refs):
    pieces, refs, out = refs[: -1 - 2 * len(picks)], refs[-1 - 2 * len(picks) : -1], refs[-1]
    tok_rows, features = out.shape
    num_experts = len(partner)
    rows = [
        piece[at : at + tok_rows]
        for piece in pieces
        for at in range(0, piece.shape[0] - tok_rows + 1, tok_rows)
    ]
    rows = jnp.concatenate(rows, axis=1)
    shares = jnp.transpose(pieces[-1][-2 * num_experts :].astype(jnp.float32))
    lanes = lax.broadcasted_iota(jnp.int32, shares.shape, 1)
    me = lax.axis_index("expert")
    other = sum(jnp.where(me == e, partner[e], 0) for e in range(num_experts))
    experts = []
    for place, which in enumerate(picks):
        gate, down = refs[2 * place], refs[2 * place + 1]
        expert = (me, other)[which]
        share = jnp.where((lanes == expert) | (lanes == expert + num_experts), shares, 0.0)
        share = jnp.sum(share, axis=1, keepdims=True)
        pre = jnp.dot(rows, gate[...], preferred_element_type=jnp.float32)
        gated, up = pre[:, :width], pre[:, width:]
        hidden = (gated / (1.0 + jnp.exp(-gated)) * up).astype(jnp.bfloat16)
        experts.append((share, hidden, down))
    columns = 4 * LANES
    for start in range(0, features, columns):
        chunk, total = slice(start, min(start + columns, features)), None
        for share, hidden, down in experts:
            part = lax.dot_general(
                hidden,
                down[chunk],
                (((1,), (1,)), ((), ())),
                preferred_element_type=jnp.float32,
            )
            part = share * part.astype(jnp.bfloat16).astype(jnp.float32)
            total = part if total is None else total + part
        out[:, chunk] = total


def finish(at, home, got, *refs):
    out, rows, done = refs[-3:]
    count = got.shape[0]
    rows[...] = (home[at : at + count] + got[...].astype(jnp.float32)).astype(rows.dtype)
    copy = pltpu.make_async_copy(rows, out.at[at : at + count], done)
    copy.start()
    copy.wait()


def ring(stops, tokens, expert_ids, route_weights, gate_up, down_t):
    tok_rows, features = tokens.shape
    num_experts, width = lax.axis_size("expert"), down_t.shape[2]
    count = len(stops)
    partner = [0] * num_experts
    onward = [0] * num_experts
    for s in range(count):
        for place, turn in ((0, 1), (1, -1)):
            partner[stops[s][place]] = stops[s][1 - place]
            onward[stops[s][place]] = stops[(s + turn) % count][place]
    hop = functools.partial(lax.ppermute, axis_name="expert", perm=list(enumerate(onward)))
    swap = functools.partial(lax.ppermute, axis_name="expert", perm=list(enumerate(partner)))
    whole = pl.BlockSpec(memory_space=pltpu.VMEM)

    given = (tokens, expert_ids.T, route_weights.T)
    given = [pltpu.with_memory_space_constraint(x, pltpu.HBM) for x in given]
    half = features // 2 // LANES * tok_rows
    packed = pl.pallas_call(
        functools.partial(pack_rows, num_experts),
        out_shape=[
            jax.ShapeDtypeStruct((rows, LANES), jnp.bfloat16)
            for rows in (half, half + 2 * num_experts)
        ],
        in_specs=[pl.BlockSpec(memory_space=pltpu.HBM)] * 3,
        out_specs=[whole] * 2,
        scratch_shapes=[pltpu.VMEM(x.shape, x.dtype) for x in given[1:]]
        + [pltpu.SemaphoreType.DMA((2 + features // LANES,))],
        compiler_params=pltpu.CompilerParams(vmem_limit_bytes=8 * 1024 * 1024),
        name="pack_rows",
    )(*given)
    away = []
    for x in packed:
        away.append(hop(x))
    own = (gate_up[0], down_t[0])
    swapped = [swap(w) for w in own]
    held = pl.pallas_call(
        load,
        out_shape=[jax.ShapeDtypeStruct(w.shape, w.dtype) for w in own],
        in_specs=[pl.BlockSpec(memory_space=pltpu.HBM)] * 2,
        out_specs=[whole] * 2,
        scratch_shapes=[pltpu.SemaphoreType.DMA((2,))],
        compiler_params=pltpu.CompilerParams(vmem_limit_bytes=2 * 1024 * 1024),
        name="load",
    )(*(pltpu.with_memory_space_constraint(w, pltpu.HBM) for w in own))
    weights = (held, swapped)

    def serve(pieces, picks):
        return pl.pallas_call(
            functools.partial(serve_rows, width, picks, partner),
            out_shape=jax.ShapeDtypeStruct((tok_rows, features), jnp.float32),
            in_specs=[whole] * (len(pieces) + 2 * len(picks)),
            out_specs=whole,
            compiler_params=pltpu.CompilerParams(vmem_limit_bytes=8 * 1024 * 1024),
            name="serve_rows",
        )(*pieces, *(w for which in picks for w in weights[which]))

    def after(arrays, other):
        return [lax.optimization_barrier((x, other))[0] for x in arrays]

    away = after(away, held)
    total = None
    for step in range(1, count):
        here = list(away)
        if step < count - 1:
            away = away if step == 1 else [jnp.concatenate(away)]
            for at, x in enumerate(away):
                away[at] = hop(x)
        more = serve(here, (0, 1))
        away = after(away, more)
        parts = 2 if step >= count - 2 else 1
        more = jnp.split(more, parts)
        if total is not None:
            if len(total) < parts:
                total = jnp.split(total[0], parts)
        sent = []
        for at, x in enumerate(more):
            if total is not None:
                y = after([total[at]], sent)[0] if parts > 1 else total[at]
                x = x + y.astype(jnp.float32)
            sent.append(x.astype(jnp.bfloat16))
        total = []
        for x in sent:
            total.append(hop(x))
    home = serve(packed, (0, 1))
    far = pl.BlockSpec(memory_space=pltpu.HBM)
    out, rows = [], tok_rows // len(total)
    for at, got in enumerate(total):
        out = [
            pl.pallas_call(
                functools.partial(finish, at * rows),
                out_shape=jax.ShapeDtypeStruct(tokens.shape, tokens.dtype),
                in_specs=[whole] * 2 + [far] * len(out),
                out_specs=far,
                input_output_aliases={2: 0} if out else {},
                scratch_shapes=[
                    pltpu.VMEM((rows, features), tokens.dtype),
                    pltpu.SemaphoreType.DMA(()),
                ],
                compiler_params=pltpu.CompilerParams(vmem_limit_bytes=4 * 1024 * 1024),
                name="finish",
            )(home, got, *out)
        ]
    return out[0]


def solution(mesh):
    placed = (
        P(("group", "expert", "token"), None),
        P(("group", "expert", "token"), None),
        P(("group", "expert", "token"), None),
        P("expert", "token", None),
        P("expert", "token", None),
    )

    stops = chip_cycle(mesh)
    cycle = mesh.shape["token"] == 1 and {len(s) for s in stops} == {2} and len(stops) > 2

    def per_device(tokens, expert_ids, route_weights, gate_up, down_t):
        fits = cycle and mesh.shape["expert"] <= 4 * expert_ids.shape[1] and gate_up.shape[0] == 1
        if fits and tokens.shape[0] == LANES and tokens.shape[1] % (2 * LANES) == 0:
            return ring(stops, tokens, expert_ids, route_weights, gate_up, down_t)
        return exchange_rows(tokens, expert_ids, route_weights, gate_up, down_t)

    return jax.shard_map(
        per_device,
        mesh=mesh,
        in_specs=placed,
        out_specs=P(("group", "expert", "token"), None),
        check_vma=False,
    )
```

```python
import functools

import jax
import jax.numpy as jnp
from jax import lax
from jax.experimental import pallas as pl
from jax.experimental.pallas import tpu as pltpu
from jax.sharding import PartitionSpec as P


def expert_apply(arrived, full_gate_up, full_down):
    shape = arrived.shape
    width = full_down.shape[2]
    rows = arrived.reshape(-1, shape[-1])
    pre = jnp.dot(rows, full_gate_up[0], preferred_element_type=jnp.float32)
    hidden = (jax.nn.silu(pre[:, :width]) * pre[:, width:]).astype(jnp.bfloat16)
    outputs = lax.dot_general(
        hidden, full_down[0], (((1,), (1,)), ((), ())), preferred_element_type=jnp.float32
    )
    return outputs.astype(jnp.bfloat16).reshape(shape)


def exchange_rows(tokens, expert_ids, route_weights, gate_up, down_t):
    tok_rows, choices_each = expert_ids.shape
    features = tokens.shape[1]
    num_experts = lax.axis_size("expert")
    slot_count = min(
        tok_rows, (3 * tok_rows * choices_each + 2 * num_experts - 1) // (2 * num_experts)
    )
    full_gate_up, full_down = (
        lax.all_gather(gate_up, "token", axis=1, tiled=True),
        lax.all_gather(down_t, "token", axis=1, tiled=True),
    )
    flat_ids = expert_ids.reshape(-1)
    onehot = (flat_ids[:, None] == jnp.arange(num_experts, dtype=jnp.int32)[None, :]).astype(
        jnp.int32
    )
    running = jnp.cumsum(onehot, axis=0)
    ranks = jnp.sum(running * onehot, axis=1) - 1
    slots = flat_ids * slot_count + ranks
    repeated = jnp.repeat(tokens, choices_each, axis=0)
    outgoing = jnp.zeros((num_experts * slot_count, features), jnp.bfloat16).at[slots].set(repeated)
    outgoing = outgoing.reshape(num_experts, slot_count, features)
    arrived = lax.all_to_all(outgoing, "expert", split_axis=0, concat_axis=0, tiled=True)
    served = expert_apply(arrived, full_gate_up, full_down)
    returned = lax.all_to_all(served, "expert", split_axis=0, concat_axis=0, tiled=True)
    picked = returned.reshape(num_experts * slot_count, features)[slots]
    picked = picked.reshape(tok_rows, choices_each, features)
    total = jnp.zeros((tok_rows, features), jnp.float32)
    for which in range(choices_each):
        total = total + route_weights[:, which : which + 1] * picked[:, which].astype(jnp.float32)
    return total.astype(jnp.bfloat16)


def chip_cycle(mesh):
    devices = mesh.devices[0, :, 0]
    chips = {}
    for index, device in enumerate(devices):
        chips.setdefault(tuple(getattr(device, "coords", (index // 2,))), []).append(index)
    coords = sorted(chips)
    wide = [d for d in range(len(coords[0])) if len({c[d] for c in coords}) > 1]
    if len(wide) == 2:
        wide.sort(key=lambda d: len({c[d] for c in coords}))
        short, long = wide
        turn = {v: i for i, v in enumerate(sorted({c[short] for c in coords}))}
        coords.sort(key=lambda c: (turn[c[short]], c[long] if turn[c[short]] % 2 == 0 else -c[long]))
    return [chips[c] for c in coords]


LANES = 128


def start_copies(pairs, done):
    copies = [pltpu.make_async_copy(a, b, done.at[i]) for i, (a, b) in enumerate(pairs)]
    for copy in copies:
        copy.start()
    return copies


def column_blocks(tokens, start, out):
    tok_rows = tokens.shape[0]
    for at in range(0, out.shape[0] - tok_rows + 1, tok_rows):
        lane = start + at // tok_rows * LANES
        yield tokens.at[:, lane : lane + LANES], out.at[at : at + tok_rows]


def pack_rows(tokens, out, done):
    for copy in start_copies(column_blocks(tokens, 0, out), done):
        copy.wait()


def pack_shares(num_experts, tokens, ids_far, weights_far, out, ids, weights, done):
    tok_rows, features = tokens.shape
    pairs = [(ids_far, ids), (weights_far, weights)]
    copies = start_copies([*pairs, *column_blocks(tokens, features // 2, out)], done)
    for copy in copies[:2]:
        copy.wait()
    place = lax.broadcasted_iota(jnp.int32, (num_experts, tok_rows), 0)
    share = jnp.zeros(place.shape, jnp.float32)
    for choice in range(ids.shape[0]):
        named = ids[choice : choice + 1] == place
        share += jnp.where(named, weights[choice : choice + 1], 0.0)
    high = share.astype(jnp.bfloat16).astype(jnp.float32)
    both = jnp.concatenate([high, share - high], axis=0)
    out[-2 * num_experts :] = both.astype(jnp.bfloat16)
    for copy in copies[2:]:
        copy.wait()


def load(*refs):
    count = len(refs) // 2
    done = refs[-1]
    copies = [pltpu.make_async_copy(refs[i], refs[count + i], done.at[i]) for i in range(count)]
    for copy in copies:
        copy.start()
    for copy in copies:
        copy.wait()


def turn_back(places, held, own, mine, rest):
    some = mine.shape[0]
    me = lax.axis_index("expert")
    place = sum(jnp.where(me == e, place, 0) for e, place in enumerate(places))

    @pl.when(place == 0)
    def _():
        mine[...] = own[:some]

    @pl.when(place != 0)
    def _():
        mine[...] = held[:some]

    rest[...] = held[some:]


def serve_rows(width, picks, partner, *refs):
    pieces, refs, out = refs[: -1 - 2 * len(picks)], refs[-1 - 2 * len(picks) : -1], refs[-1]
    tok_rows, features = out.shape
    num_experts = len(partner)
    rows = [
        piece[at : at + tok_rows]
        for piece in pieces
        for at in range(0, piece.shape[0] - tok_rows + 1, tok_rows)
    ]
    rows = jnp.concatenate(rows, axis=1)
    shares = jnp.transpose(pieces[-1][-2 * num_experts :].astype(jnp.float32))
    lanes = lax.broadcasted_iota(jnp.int32, shares.shape, 1)
    me = lax.axis_index("expert")
    other = sum(jnp.where(me == e, partner[e], 0) for e in range(num_experts))
    experts = []
    for place, which in enumerate(picks):
        gate, down = refs[2 * place], refs[2 * place + 1]
        expert = (me, other)[which]
        share = jnp.where((lanes == expert) | (lanes == expert + num_experts), shares, 0.0)
        share = jnp.sum(share, axis=1, keepdims=True)
        pre = jnp.dot(rows, gate[...], preferred_element_type=jnp.float32)
        gated, up = pre[:, :width], pre[:, width:]
        hidden = (gated / (1.0 + jnp.exp(-gated)) * up).astype(jnp.bfloat16)
        experts.append((share, hidden, down))
    columns = 4 * LANES
    for start in range(0, features, columns):
        chunk, total = slice(start, min(start + columns, features)), None
        for share, hidden, down in experts:
            part = lax.dot_general(
                hidden,
                down[chunk],
                (((1,), (1,)), ((), ())),
                preferred_element_type=jnp.float32,
            )
            part = share * part.astype(jnp.bfloat16).astype(jnp.float32)
            total = part if total is None else total + part
        out[:, chunk] = total


def finish(at, home, got, *refs):
    out, rows, done = refs[-3:]
    count = got.shape[0]
    rows[...] = (home[at : at + count] + got[...].astype(jnp.float32)).astype(rows.dtype)
    copy = pltpu.make_async_copy(rows, out.at[at : at + count], done)
    copy.start()
    copy.wait()


def ring(stops, tokens, expert_ids, route_weights, gate_up, down_t):
    tok_rows, features = tokens.shape
    num_experts, width = lax.axis_size("expert"), down_t.shape[2]
    count = len(stops)
    partner = [0] * num_experts
    onward = [0] * num_experts
    back = [0] * num_experts
    places = [0] * num_experts
    for s in range(count):
        for place, turn in ((0, 1), (1, -1)):
            partner[stops[s][place]] = stops[s][1 - place]
            onward[stops[s][place]] = stops[(s + turn) % count][place]
            back[stops[s][place]] = stops[(s - 1) % count][place]
            places[stops[s][place]] = place
    hop = functools.partial(lax.ppermute, axis_name="expert", perm=list(enumerate(onward)))
    swap = functools.partial(lax.ppermute, axis_name="expert", perm=list(enumerate(partner)))
    whole = pl.BlockSpec(memory_space=pltpu.VMEM)

    far = pl.BlockSpec(memory_space=pltpu.HBM)
    given = (tokens, expert_ids.T, route_weights.T)
    given = [pltpu.with_memory_space_constraint(x, pltpu.HBM) for x in given]
    half = features // 2 // LANES * tok_rows
    blocks = half // tok_rows
    small = pltpu.CompilerParams(vmem_limit_bytes=4 * 1024 * 1024)
    packed = [
        pl.pallas_call(
            pack_rows,
            out_shape=jax.ShapeDtypeStruct((half, LANES), jnp.bfloat16),
            in_specs=[far],
            out_specs=whole,
            scratch_shapes=[pltpu.SemaphoreType.DMA((blocks,))],
            compiler_params=small,
            name="pack_rows",
        )(given[0])
    ]
    packed.append(
        pl.pallas_call(
            functools.partial(pack_shares, num_experts),
            out_shape=jax.ShapeDtypeStruct((half + 2 * num_experts, LANES), jnp.bfloat16),
            in_specs=[far] * 3,
            out_specs=whole,
            scratch_shapes=[pltpu.VMEM(x.shape, x.dtype) for x in given[1:]]
            + [pltpu.SemaphoreType.DMA((2 + blocks,))],
            compiler_params=small,
            name="pack_shares",
        )(*given)
    )
    away = []
    for x in packed:
        away.append(hop(x))
    own = (gate_up[0], down_t[0])
    swapped = [swap(w) for w in own]
    held = pl.pallas_call(
        load,
        out_shape=[jax.ShapeDtypeStruct(w.shape, w.dtype) for w in own],
        in_specs=[pl.BlockSpec(memory_space=pltpu.HBM)] * 2,
        out_specs=[whole] * 2,
        scratch_shapes=[pltpu.SemaphoreType.DMA((2,))],
        compiler_params=pltpu.CompilerParams(vmem_limit_bytes=2 * 1024 * 1024),
        name="load",
    )(*(pltpu.with_memory_space_constraint(w, pltpu.HBM) for w in own))
    weights = (held, swapped)

    def serve(pieces, picks):
        return pl.pallas_call(
            functools.partial(serve_rows, width, picks, partner),
            out_shape=jax.ShapeDtypeStruct((tok_rows, features), jnp.float32),
            in_specs=[whole] * (len(pieces) + 2 * len(picks)),
            out_specs=whole,
            compiler_params=pltpu.CompilerParams(vmem_limit_bytes=8 * 1024 * 1024),
            name="serve_rows",
        )(*pieces, *(w for which in picks for w in weights[which]))

    def after(arrays, other):
        return [lax.optimization_barrier((x, other))[0] for x in arrays]

    away = after(away, held)
    some = features // LANES * 5 // 16 * tok_rows
    total = None
    for step in range(1, count):
        here = list(away)
        if step < count - 1:
            away = away if step == 1 else [jnp.concatenate(away)]
            if step == count - 2:
                mine, rest = pl.pallas_call(
                    functools.partial(turn_back, places),
                    out_shape=[
                        jax.ShapeDtypeStruct((rows, LANES), jnp.bfloat16)
                        for rows in (some, away[0].shape[0] - some)
                    ],
                    in_specs=[whole] * 2,
                    out_specs=[whole] * 2,
                    compiler_params=pltpu.CompilerParams(vmem_limit_bytes=2 * 1024 * 1024),
                    name="turn_back",
                )(away[0], packed[0])
                away = [lax.ppermute(mine, "expert", list(enumerate(back))), hop(rest)]
            else:
                for at, x in enumerate(away):
                    away[at] = hop(x)
        more = serve(here, (0, 1))
        away = after(away, more)
        parts = 2 if step >= count - 2 else 1
        more = jnp.split(more, parts)
        if total is not None:
            if len(total) < parts:
                total = jnp.split(total[0], parts)
        sent = []
        for at, x in enumerate(more):
            if total is not None:
                y = after([total[at]], sent)[0] if parts > 1 else total[at]
                x = x + y.astype(jnp.float32)
            sent.append(x.astype(jnp.bfloat16))
        total = []
        for x in sent:
            total.append(hop(x))
    home = serve(packed, (0, 1))
    far = pl.BlockSpec(memory_space=pltpu.HBM)
    out, rows = [], tok_rows // len(total)
    for at, got in enumerate(total):
        out = [
            pl.pallas_call(
                functools.partial(finish, at * rows),
                out_shape=jax.ShapeDtypeStruct(tokens.shape, tokens.dtype),
                in_specs=[whole] * 2 + [far] * len(out),
                out_specs=far,
                input_output_aliases={2: 0} if out else {},
                scratch_shapes=[
                    pltpu.VMEM((rows, features), tokens.dtype),
                    pltpu.SemaphoreType.DMA(()),
                ],
                compiler_params=pltpu.CompilerParams(vmem_limit_bytes=4 * 1024 * 1024),
                name="finish",
            )(home, got, *out)
        ]
    return out[0]


def solution(mesh):
    placed = (
        P(("group", "expert", "token"), None),
        P(("group", "expert", "token"), None),
        P(("group", "expert", "token"), None),
        P("expert", "token", None),
        P("expert", "token", None),
    )

    stops = chip_cycle(mesh)
    cycle = mesh.shape["token"] == 1 and {len(s) for s in stops} == {2} and len(stops) > 4

    def per_device(tokens, expert_ids, route_weights, gate_up, down_t):
        fits = cycle and mesh.shape["expert"] <= 4 * expert_ids.shape[1] and gate_up.shape[0] == 1
        if fits and tokens.shape[0] == LANES and tokens.shape[1] % (2 * LANES) == 0:
            return ring(stops, tokens, expert_ids, route_weights, gate_up, down_t)
        return exchange_rows(tokens, expert_ids, route_weights, gate_up, down_t)

    return jax.shard_map(
        per_device,
        mesh=mesh,
        in_specs=placed,
        out_specs=P(("group", "expert", "token"), None),
        check_vma=False,
    )
```

```python
import functools

import jax
import jax.numpy as jnp
from jax import lax
from jax.experimental import pallas as pl
from jax.experimental.pallas import tpu as pltpu
from jax.sharding import PartitionSpec as P


def expert_apply(arrived, full_gate_up, full_down):
    shape = arrived.shape
    width = full_down.shape[2]
    rows = arrived.reshape(-1, shape[-1])
    pre = jnp.dot(rows, full_gate_up[0], preferred_element_type=jnp.float32)
    hidden = (jax.nn.silu(pre[:, :width]) * pre[:, width:]).astype(jnp.bfloat16)
    outputs = lax.dot_general(
        hidden, full_down[0], (((1,), (1,)), ((), ())), preferred_element_type=jnp.float32
    )
    return outputs.astype(jnp.bfloat16).reshape(shape)


def exchange_rows(tokens, expert_ids, route_weights, gate_up, down_t):
    tok_rows, choices_each = expert_ids.shape
    features = tokens.shape[1]
    num_experts = lax.axis_size("expert")
    slot_count = min(
        tok_rows, (3 * tok_rows * choices_each + 2 * num_experts - 1) // (2 * num_experts)
    )
    full_gate_up, full_down = (
        lax.all_gather(gate_up, "token", axis=1, tiled=True),
        lax.all_gather(down_t, "token", axis=1, tiled=True),
    )
    flat_ids = expert_ids.reshape(-1)
    onehot = (flat_ids[:, None] == jnp.arange(num_experts, dtype=jnp.int32)[None, :]).astype(
        jnp.int32
    )
    running = jnp.cumsum(onehot, axis=0)
    ranks = jnp.sum(running * onehot, axis=1) - 1
    slots = flat_ids * slot_count + ranks
    repeated = jnp.repeat(tokens, choices_each, axis=0)
    outgoing = jnp.zeros((num_experts * slot_count, features), jnp.bfloat16).at[slots].set(repeated)
    outgoing = outgoing.reshape(num_experts, slot_count, features)
    arrived = lax.all_to_all(outgoing, "expert", split_axis=0, concat_axis=0, tiled=True)
    served = expert_apply(arrived, full_gate_up, full_down)
    returned = lax.all_to_all(served, "expert", split_axis=0, concat_axis=0, tiled=True)
    picked = returned.reshape(num_experts * slot_count, features)[slots]
    picked = picked.reshape(tok_rows, choices_each, features)
    total = jnp.zeros((tok_rows, features), jnp.float32)
    for which in range(choices_each):
        total = total + route_weights[:, which : which + 1] * picked[:, which].astype(jnp.float32)
    return total.astype(jnp.bfloat16)


def chip_cycle(mesh):
    devices = mesh.devices[0, :, 0]
    chips = {}
    for index, device in enumerate(devices):
        chips.setdefault(tuple(getattr(device, "coords", (index // 2,))), []).append(index)
    coords = sorted(chips)
    wide = [d for d in range(len(coords[0])) if len({c[d] for c in coords}) > 1]
    if len(wide) == 2:
        wide.sort(key=lambda d: len({c[d] for c in coords}))
        short, long = wide
        turn = {v: i for i, v in enumerate(sorted({c[short] for c in coords}))}
        coords.sort(key=lambda c: (turn[c[short]], c[long] if turn[c[short]] % 2 == 0 else -c[long]))
    return [chips[c] for c in coords]


LANES = 128


def pack_rows(num_experts, tokens, ids_far, weights_far, out_a, out_b, ids, weights, done):
    outs = (out_a, out_b)
    tok_rows, features = tokens.shape
    half = features // 2
    pairs = [(ids_far, ids), (weights_far, weights)]
    for start in range(0, features, LANES):
        at = start % half // LANES * tok_rows
        pairs.append(
            (tokens.at[:, start : start + LANES], outs[start // half].at[at : at + tok_rows])
        )
    copies = [pltpu.make_async_copy(a, b, done.at[i]) for i, (a, b) in enumerate(pairs)]
    for copy in copies:
        copy.start()
    for copy in copies[:2]:
        copy.wait()
    place = lax.broadcasted_iota(jnp.int32, (num_experts, tok_rows), 0)
    share = jnp.zeros(place.shape, jnp.float32)
    for choice in range(ids.shape[0]):
        named = ids[choice : choice + 1] == place
        share += jnp.where(named, weights[choice : choice + 1], 0.0)
    high = share.astype(jnp.bfloat16).astype(jnp.float32)
    both = jnp.concatenate([high, share - high], axis=0)
    out_b[half // LANES * tok_rows :] = both.astype(jnp.bfloat16)
    for copy in copies[2:]:
        copy.wait()


def load(*refs):
    count = len(refs) // 2
    done = refs[-1]
    copies = [pltpu.make_async_copy(refs[i], refs[count + i], done.at[i]) for i in range(count)]
    for copy in copies:
        copy.start()
    for copy in copies:
        copy.wait()


def turn_back(places, held, own, mine, rest):
    some = mine.shape[0]
    me = lax.axis_index("expert")
    place = sum(jnp.where(me == e, place, 0) for e, place in enumerate(places))

    @pl.when(place == 0)
    def _():
        mine[...] = own[:some]

    @pl.when(place != 0)
    def _():
        mine[...] = held[:some]

    rest[...] = held[some:]


def serve_rows(width, picks, partner, *refs):
    pieces, refs, out = refs[: -1 - 2 * len(picks)], refs[-1 - 2 * len(picks) : -1], refs[-1]
    tok_rows, features = out.shape
    num_experts = len(partner)
    rows = [
        piece[at : at + tok_rows]
        for piece in pieces
        for at in range(0, piece.shape[0] - tok_rows + 1, tok_rows)
    ]
    rows = jnp.concatenate(rows, axis=1)
    shares = jnp.transpose(pieces[-1][-2 * num_experts :].astype(jnp.float32))
    lanes = lax.broadcasted_iota(jnp.int32, shares.shape, 1)
    me = lax.axis_index("expert")
    other = sum(jnp.where(me == e, partner[e], 0) for e in range(num_experts))
    experts = []
    for place, which in enumerate(picks):
        gate, down = refs[2 * place], refs[2 * place + 1]
        expert = (me, other)[which]
        share = jnp.where((lanes == expert) | (lanes == expert + num_experts), shares, 0.0)
        share = jnp.sum(share, axis=1, keepdims=True)
        pre = jnp.dot(rows, gate[...], preferred_element_type=jnp.float32)
        gated, up = pre[:, :width], pre[:, width:]
        hidden = (gated / (1.0 + jnp.exp(-gated)) * up).astype(jnp.bfloat16)
        experts.append((share, hidden, down))
    columns = 2 * LANES
    for start in range(0, features, columns):
        chunk, total = slice(start, min(start + columns, features)), None
        for share, hidden, down in experts:
            part = lax.dot_general(
                hidden,
                down[chunk],
                (((1,), (1,)), ((), ())),
                preferred_element_type=jnp.float32,
            )
            part = share * part.astype(jnp.bfloat16).astype(jnp.float32)
            total = part if total is None else total + part
        out[:, chunk] = total


def finish(at, home, got, *refs):
    out, rows, done = refs[-3:]
    count = got.shape[0]
    rows[...] = (home[at : at + count] + got[...].astype(jnp.float32)).astype(rows.dtype)
    copy = pltpu.make_async_copy(rows, out.at[at : at + count], done)
    copy.start()
    copy.wait()


def ring(stops, tokens, expert_ids, route_weights, gate_up, down_t):
    tok_rows, features = tokens.shape
    num_experts, width = lax.axis_size("expert"), down_t.shape[2]
    count = len(stops)
    partner = [0] * num_experts
    onward = [0] * num_experts
    back = [0] * num_experts
    places = [0] * num_experts
    for s in range(count):
        for place, turn in ((0, 1), (1, -1)):
            partner[stops[s][place]] = stops[s][1 - place]
            onward[stops[s][place]] = stops[(s + turn) % count][place]
            back[stops[s][place]] = stops[(s - 1) % count][place]
            places[stops[s][place]] = place
    hop = functools.partial(lax.ppermute, axis_name="expert", perm=list(enumerate(onward)))
    swap = functools.partial(lax.ppermute, axis_name="expert", perm=list(enumerate(partner)))
    whole = pl.BlockSpec(memory_space=pltpu.VMEM)

    given = (tokens, expert_ids.T, route_weights.T)
    given = [pltpu.with_memory_space_constraint(x, pltpu.HBM) for x in given]
    half = features // 2 // LANES * tok_rows
    packed = pl.pallas_call(
        functools.partial(pack_rows, num_experts),
        out_shape=[
            jax.ShapeDtypeStruct((rows, LANES), jnp.bfloat16)
            for rows in (half, half + 2 * num_experts)
        ],
        in_specs=[pl.BlockSpec(memory_space=pltpu.HBM)] * 3,
        out_specs=[whole] * 2,
        scratch_shapes=[pltpu.VMEM(x.shape, x.dtype) for x in given[1:]]
        + [pltpu.SemaphoreType.DMA((2 + features // LANES,))],
        compiler_params=pltpu.CompilerParams(vmem_limit_bytes=8 * 1024 * 1024),
        name="pack_rows",
    )(*given)
    away = []
    for x in packed:
        away.append(hop(x))
    own = (gate_up[0], down_t[0])
    swapped = [swap(w) for w in own]
    held = pl.pallas_call(
        load,
        out_shape=[jax.ShapeDtypeStruct(w.shape, w.dtype) for w in own],
        in_specs=[pl.BlockSpec(memory_space=pltpu.HBM)] * 2,
        out_specs=[whole] * 2,
        scratch_shapes=[pltpu.SemaphoreType.DMA((2,))],
        compiler_params=pltpu.CompilerParams(vmem_limit_bytes=2 * 1024 * 1024),
        name="load",
    )(*(pltpu.with_memory_space_constraint(w, pltpu.HBM) for w in own))
    weights = (held, swapped)

    def serve(pieces, picks):
        return pl.pallas_call(
            functools.partial(serve_rows, width, picks, partner),
            out_shape=jax.ShapeDtypeStruct((tok_rows, features), jnp.float32),
            in_specs=[whole] * (len(pieces) + 2 * len(picks)),
            out_specs=whole,
            compiler_params=pltpu.CompilerParams(vmem_limit_bytes=8 * 1024 * 1024),
            name="serve_rows",
        )(*pieces, *(w for which in picks for w in weights[which]))

    def after(arrays, other):
        return [lax.optimization_barrier((x, other))[0] for x in arrays]

    away = after(away, held)
    some = features // LANES * 5 // 16 * tok_rows
    total = None
    for step in range(1, count):
        here = list(away)
        if step < count - 1:
            away = away if step == 1 else [jnp.concatenate(away)]
            if step == count - 2:
                mine, rest = pl.pallas_call(
                    functools.partial(turn_back, places),
                    out_shape=[
                        jax.ShapeDtypeStruct((rows, LANES), jnp.bfloat16)
                        for rows in (some, away[0].shape[0] - some)
                    ],
                    in_specs=[whole] * 2,
                    out_specs=[whole] * 2,
                    compiler_params=pltpu.CompilerParams(vmem_limit_bytes=2 * 1024 * 1024),
                    name="turn_back",
                )(away[0], packed[0])
                away = [lax.ppermute(mine, "expert", list(enumerate(back))), hop(rest)]
            else:
                for at, x in enumerate(away):
                    away[at] = hop(x)
        more = serve(here, (0, 1))
        away = after(away, more)
        parts = 2 if step >= count - 2 else 1
        more = jnp.split(more, parts)
        if total is not None:
            if len(total) < parts:
                total = jnp.split(total[0], parts)
        sent = []
        for at, x in enumerate(more):
            if total is not None:
                y = after([total[at]], sent)[0] if parts > 1 else total[at]
                x = x + y.astype(jnp.float32)
            sent.append(x.astype(jnp.bfloat16))
        total = []
        for x in sent:
            total.append(hop(x))
    home = serve(packed, (0, 1))
    far = pl.BlockSpec(memory_space=pltpu.HBM)
    out, rows = [], tok_rows // len(total)
    for at, got in enumerate(total):
        out = [
            pl.pallas_call(
                functools.partial(finish, at * rows),
                out_shape=jax.ShapeDtypeStruct(tokens.shape, tokens.dtype),
                in_specs=[whole] * 2 + [far] * len(out),
                out_specs=far,
                input_output_aliases={2: 0} if out else {},
                scratch_shapes=[
                    pltpu.VMEM((rows, features), tokens.dtype),
                    pltpu.SemaphoreType.DMA(()),
                ],
                compiler_params=pltpu.CompilerParams(vmem_limit_bytes=4 * 1024 * 1024),
                name="finish",
            )(home, got, *out)
        ]
    return out[0]


def solution(mesh):
    placed = (
        P(("group", "expert", "token"), None),
        P(("group", "expert", "token"), None),
        P(("group", "expert", "token"), None),
        P("expert", "token", None),
        P("expert", "token", None),
    )

    stops = chip_cycle(mesh)
    cycle = mesh.shape["token"] == 1 and {len(s) for s in stops} == {2} and len(stops) > 4

    def per_device(tokens, expert_ids, route_weights, gate_up, down_t):
        fits = cycle and mesh.shape["expert"] <= 4 * expert_ids.shape[1] and gate_up.shape[0] == 1
        if fits and tokens.shape[0] == LANES and tokens.shape[1] % (2 * LANES) == 0:
            return ring(stops, tokens, expert_ids, route_weights, gate_up, down_t)
        return exchange_rows(tokens, expert_ids, route_weights, gate_up, down_t)

    return jax.shard_map(
        per_device,
        mesh=mesh,
        in_specs=placed,
        out_specs=P(("group", "expert", "token"), None),
        check_vma=False,
    )
```
